512 devices in a mesh: dom: 128 (over z, y, core), feat: 4 (over x).
Axes of the slice: x: 4, y: 4, z: 16, core: 2. Of those that a mesh axis runs over, the one named last changes fastest.
Arguments:
- edge_feats: bfloat16 [65536, 1024], P('dom', 'feat'), may hold values from -6 to 6
- cotangent: bfloat16 [65536, 1024], P('dom', 'feat'), may hold values from -6 to 6
- w_down: bfloat16 [1024, 128], P('feat'), may hold values from -0.1875 to 0.1875
- w_up: bfloat16 [128, 1024], P(None, 'feat'), may hold values from -0.5 to 0.5
- w_bil: bfloat16 [4096, 128], replicated, may hold values from -0.09375 to 0.09375
- basis: float32 [16, 32, 65536], P(None, None, 'dom'), may hold values from -3 to 3
- trip_k: int32 [65536, 16], P('dom'), may hold values from 0 to 1279, as said below
- trip_count: int32 [65536], P('dom'), may hold values from 1 to 16, as said below
- send_rows: int32 [128, 6, 128], P('dom'), may hold values from 0 to 511, as said below
Outputs:
- input_grad: bfloat16 [65536, 1024], P('dom', 'feat')
- w_down_grad: float32 [1024, 128], P('feat')
- w_up_grad: float32 [128, 1024], P(None, 'feat')
- w_bil_grad: float32 [4096, 128], P('feat')
The draws below stay inside these ranges and needn't reach their ends.
Inputs may be any that keep to these rules, and one draw needn't show every extreme that they name: `send_rows`: entry [p, j, s] is an edge of domain p (a row of its 512) placed in slot s of p's block for domain (p + o(j)) mod 128. The filled slots of a block come first and hold distinct edges; every block has one to 128 filled slots; some domain receives 128 filled slots from each of its neighbours; empty slots hold 0. `trip_k`: each entry is a row of the extended table of the edge's own domain: below 512 its own edges, else row 512 + j * 128 + s, which is always a filled slot of the block that the domain receives from its neighbour j. `trip_count`: the live triplets of an edge are its first ones; every domain has an edge with all 16 live.
All inputs are finite; a program needn't handle non-finite values.
Results may differ from the reference program's by a relative error of at most 0.012.
Values may be sent and summed in bfloat16 or wider, within the bound.
No kernel may reach another device: no remote copies, remote signals or barrier semaphores. Data moves between devices by JAX's collectives and lax.ppermute only.
A program may use at most 64 MiB of HBM per device.

```python
import math
import jax
import jax.numpy as jnp
from jax import lax

D = 1024
DT = 128
NB = 32
TRIPS_PER_EDGE = 16
REACH = 3
SLOT = 128
EDGE_DEV = 512
EDGES = 65536
N_DOM = 128


def block_offsets():
    steps_out = jnp.arange(1, REACH + 1, dtype=jnp.int32)
    return jnp.concatenate([steps_out, -steps_out])


def slot_table(key):
    base_key = jax.random.fold_in(key, 7001)
    lowest = max(1, SLOT // 3)
    table = jax.random.randint(jax.random.fold_in(base_key, 1), (N_DOM, 2 * REACH), lowest, SLOT + 1)
    full_holder = jax.random.randint(jax.random.fold_in(base_key, 2), (), 0, N_DOM)
    holders = jnp.arange(N_DOM)
    table = jnp.where(holders[:, None] == full_holder, SLOT, table)
    return table.astype(jnp.int32)


def draw_send_rows(key, part):
    table = slot_table(key)
    offsets = block_offsets()
    targets = (jnp.arange(N_DOM)[:, None] + offsets[None, :]) % N_DOM
    sent_count = jnp.take_along_axis(table[targets, :], jnp.arange(2 * REACH)[None, :, None], axis=2)[:, :, 0]
    first_row = jax.random.randint(jax.random.fold_in(key, 7002), (N_DOM, 2 * REACH, 1), 0, EDGE_DEV)
    row_ids = (first_row + jnp.arange(SLOT)[None, None, :] * (EDGE_DEV // SLOT)) % EDGE_DEV
    filled = jnp.arange(SLOT)[None, None, :] < sent_count[:, :, None]
    return jnp.where(filled, row_ids, 0).astype(jnp.int32)


def draw_trip_k(key, part):
    table = slot_table(key)
    base_key = jax.random.fold_in(key, 7003)
    pick_shape = (N_DOM, EDGE_DEV * TRIPS_PER_EDGE)
    totals = jnp.sum(table, axis=1, keepdims=True)
    draw_pick = jax.random.randint(jax.random.fold_in(base_key, 1), pick_shape, 0, EDGE_DEV + totals)
    cum_end = jnp.cumsum(table, axis=1)
    cum_start = cum_end - table
    remote_index = draw_pick - EDGE_DEV
    block_pick = jnp.sum((remote_index[:, :, None] >= cum_end[:, None, :]).astype(jnp.int32), axis=2)
    block_pick = jnp.minimum(block_pick, 2 * REACH - 1)
    block_start = jnp.take_along_axis(cum_start, block_pick, axis=1)
    slot_pick = remote_index - block_start
    remote_pick = EDGE_DEV + block_pick * SLOT + slot_pick
    chosen = jnp.where(draw_pick < EDGE_DEV, draw_pick, remote_pick)
    return chosen.reshape(EDGES, TRIPS_PER_EDGE).astype(jnp.int32)


def draw_trip_count(key, part):
    base_key = jax.random.fold_in(key, 7004)
    lowest = jax.random.randint(jax.random.fold_in(base_key, 1), (N_DOM, 1), 1, TRIPS_PER_EDGE + 1)
    live_counts = jax.random.randint(jax.random.fold_in(base_key, 2), (N_DOM, EDGE_DEV), lowest, TRIPS_PER_EDGE + 1)
    full_edge = jax.random.randint(jax.random.fold_in(base_key, 3), (N_DOM, 1), 0, EDGE_DEV)
    live_counts = jnp.where(jnp.arange(EDGE_DEV)[None, :] == full_edge, TRIPS_PER_EDGE, live_counts)
    return live_counts.reshape(EDGES).astype(jnp.int32)


def levels(own_key, dims, shards, least, high):
    def one(position, shards_of):
        steps = jax.random.uniform(jax.random.fold_in(jax.random.fold_in(own_key, 6), position), (shards_of,), jnp.float32, least / len(shards), high / len(shards))
        return jnp.repeat(jnp.exp(steps), dims[position] // shards_of).reshape((-1,) + (1,) * (len(dims) - position - 1))

    level = one(*shards[0])
    for cut in shards[1:]:
        level = level * one(*cut)
    return level


def scatter_about(own_key, dims, spread, reach, pieces=(), kind=jnp.bfloat16):
    gain = levels(own_key, dims, pieces, -0.22, 0.18) if pieces else 1.0
    entries = jax.random.normal(own_key, dims, jnp.float32) * spread * gain
    return jnp.minimum(jnp.maximum(entries, -reach), reach).astype(kind)


def setup_inputs(seed: int = 0) -> dict:
    keys = jax.random.split(jax.random.key(seed), 10)
    return {
        "edge_feats": scatter_about(keys[0], (EDGES, D), 1.0, 6.0, ((0, 128), (1, 4))),
        "cotangent": scatter_about(keys[1], (EDGES, D), 1.0, 6.0, ((0, 128), (1, 4))),
        "w_down": scatter_about(keys[2], (D, DT), D ** -0.5, 0.1875, ((0, 4),)),
        "w_up": scatter_about(keys[3], (DT, D), DT ** -0.5, 0.5, ((1, 4),)),
        "w_bil": scatter_about(keys[4], (NB * DT, DT), (NB * DT) ** -0.5, 0.09375),
        "basis": scatter_about(keys[5], (TRIPS_PER_EDGE, NB, EDGES), 0.5, 3.0, ((2, 128),), jnp.float32),
        "trip_k": draw_trip_k(jax.random.fold_in(keys[9], 71), 0),
        "trip_count": draw_trip_count(jax.random.fold_in(keys[9], 71), 0),
        "send_rows": draw_send_rows(jax.random.fold_in(keys[9], 71), 0),
    }


ALONG_ROWS = (((1,), (1,)), ((), ()))
ALONG_COLS = (((0,), (0,)), ((), ()))

def silu_grad(value):
    sigma = jax.nn.sigmoid(value)
    return sigma * (1.0 + value * (1.0 - sigma))

def reference(edge_feats, cotangent, w_down, w_up, w_bil, basis, trip_k, trip_count, send_rows):
    preact = jnp.dot(edge_feats, w_down, preferred_element_type=jnp.float32)
    down_rows = jax.nn.silu(preact).astype(jnp.bfloat16)
    agg_bar = lax.dot_general(cotangent, w_up, ALONG_ROWS, preferred_element_type=jnp.float32).astype(jnp.bfloat16)
    owners = jnp.arange(N_DOM, dtype=jnp.int32)
    steps_out = jnp.arange(1, REACH + 1, dtype=jnp.int32)
    offsets = jnp.concatenate([steps_out, -steps_out]).astype(jnp.int32)
    senders = ((owners[:, None] - offsets[None, :]) % N_DOM).astype(jnp.int32)
    block_ids = jnp.arange(2 * REACH, dtype=jnp.int32)
    picked = send_rows[senders, block_ids[None, :]]
    remote_rows = (senders[:, :, None] * EDGE_DEV + picked).astype(jnp.int32).reshape(N_DOM, 2 * REACH * SLOT)
    local_rows = owners[:, None] * EDGE_DEV + jnp.arange(EDGE_DEV, dtype=jnp.int32)[None, :]
    ext_rows = jnp.concatenate([local_rows, remote_rows], axis=1).astype(jnp.int32)
    live_mask = (jnp.arange(TRIPS_PER_EDGE, dtype=jnp.int32)[:, None] < trip_count[None, :]).astype(jnp.float32)
    weights = basis * live_mask[:, None, :]

    def holder(state_pair, domain):
        d_down, bil_total = state_pair
        first_row = (domain * EDGE_DEV).astype(jnp.int32)
        pick_rows = lax.dynamic_slice_in_dim(trip_k, first_row, EDGE_DEV, 0)
        ext_table = lax.dynamic_index_in_dim(ext_rows, domain, 0, keepdims=False)
        sources_k = jnp.take(ext_table, pick_rows, axis=0).astype(jnp.int32)
        gathered = jnp.take(down_rows, sources_k, axis=0).astype(jnp.float32)
        local_weights = lax.dynamic_slice_in_dim(weights, first_row, EDGE_DEV, 2)
        summed = jnp.einsum('knE,Ekc->Enc', local_weights, gathered)
        summed = summed.reshape(EDGE_DEV, NB * DT).astype(jnp.bfloat16)
        aggregate = jnp.dot(summed, w_bil, preferred_element_type=jnp.float32)
        bar_rows = lax.dynamic_slice_in_dim(agg_bar, first_row, EDGE_DEV, 0)
        grad_in = lax.dot_general(bar_rows, w_bil, ALONG_ROWS, preferred_element_type=jnp.float32)
        grad_in = lax.optimization_barrier(grad_in.astype(jnp.bfloat16)).astype(jnp.float32)
        grad_in = grad_in.reshape(EDGE_DEV, NB, DT)
        d_gathered = jnp.einsum('knE,Enc->Ekc', local_weights, grad_in)
        d_down = d_down.at[sources_k.reshape(-1)].add(d_gathered.reshape(-1, DT))
        bil_total = bil_total + lax.dot_general(summed, bar_rows, ALONG_COLS, preferred_element_type=jnp.float32)
        return ((d_down, bil_total), aggregate)
    start_state = (jnp.zeros((EDGES, DT), jnp.float32), jnp.zeros((NB * DT, DT), jnp.float32))
    (d_down, bil_total), aggregates = lax.scan(holder, start_state, owners)
    aggregate = aggregates.reshape(EDGES, DT)
    pre_bar = (d_down * silu_grad(preact)).astype(jnp.bfloat16)
    input_grad = (cotangent.astype(jnp.float32) + lax.dot_general(pre_bar, w_down, ALONG_ROWS, preferred_element_type=jnp.float32)).astype(jnp.bfloat16)
    factor = 1.0 / math.sqrt(EDGES)
    w_down_grad = lax.dot_general(edge_feats, pre_bar, ALONG_COLS, preferred_element_type=jnp.float32) * factor
    agg_low = aggregate.astype(jnp.bfloat16)
    w_up_grad = lax.dot_general(agg_low, cotangent, ALONG_COLS, preferred_element_type=jnp.float32) * factor
    w_bil_grad = bil_total * factor
    return (input_grad, w_down_grad, w_up_grad, w_bil_grad)
```

```python
import functools
import math

import jax
import jax.numpy as jnp
from jax import lax
from jax.experimental import pallas as pl
from jax.experimental.pallas import tpu as pltpu
from jax.sharding import Mesh
from jax.sharding import PartitionSpec as P

BF = jnp.bfloat16
F32 = jnp.float32
NT = (((1,), (1,)), ((), ()))
TN = (((0,), (0,)), ((), ()))
DOM = ("zh", "zl", "y", "core")
GROUP = 16


def dot(a, b, dims=(((1,), (0,)), ((), ()))):
    return lax.dot_general(a, b, dims, preferred_element_type=F32)


def ones_where(cond):
    return jnp.where(cond, 1.0, 0.0).astype(BF)


def iota(shape, dim):
    return lax.broadcasted_iota(jnp.int32, shape, dim)


def silu_grad(value):
    sigma = jax.nn.sigmoid(value)
    return sigma * (1.0 + value * (1.0 - sigma))


def call(kernel, outs, scratch, flops, *args):
    moved = sum(a.size * a.dtype.itemsize for a in args)
    return pl.pallas_call(
        kernel,
        out_shape=outs,
        scratch_shapes=scratch,
        compiler_params=pltpu.CompilerParams(vmem_limit_bytes=40 << 20),
        cost_estimate=pl.CostEstimate(flops=flops, bytes_accessed=moved, transcendentals=0),
    )(*args)


def down_kernel(pre_ref, send_ref, down_ref, *out_refs):
    pre = pre_ref[...].astype(F32)
    down = (pre * jax.nn.sigmoid(pre)).astype(BF)
    down_ref[...] = down
    slots = out_refs[0].shape[0]
    edges = down.shape[0]
    for j, out_ref in enumerate(out_refs):
        pick = ones_where(send_ref[j * slots : (j + 1) * slots, :] == iota((slots, edges), 1))
        out_ref[...] = dot(pick, down).astype(BF)


def back_kernel(bar_ref, wbil_ref, w_ref, k_ref, own_ref, *rest):
    rem_refs, grad_ref, mask_ref, acc_ref = rest[:-3], *rest[-3:]
    basis, edges, width = grad_ref.shape
    trips = w_ref.shape[0]
    rows, cols = trips * GROUP, basis * GROUP
    table = acc_ref.shape[0]
    bar = bar_ref[...]
    for b in range(basis):
        grad_ref[b] = dot(bar, wbil_ref[b * width : (b + 1) * width, :], NT).astype(BF)
    mask_ref[...] = ones_where(iota((rows, cols), 0) % GROUP == iota((rows, cols), 1) % GROUP)
    spread = ones_where(iota((basis, cols), 0) == iota((basis, cols), 1) // GROUP)
    acc_ref[...] = jnp.zeros_like(acc_ref)

    def body(g, carry):
        at = pl.ds(pl.multiple_of(g * GROUP, GROUP), GROUP)
        w = w_ref[:, at, :].reshape(rows, basis)
        diag = dot(w, spread).astype(BF) * mask_ref[...]
        grad = grad_ref[:, at, :].reshape(cols, width)
        d_rows = dot(diag, grad).astype(BF)
        pick = ones_where(k_ref[g] == iota((table, rows), 0))
        acc_ref[...] += dot(pick, d_rows)
        return carry

    lax.fori_loop(0, edges // GROUP, body, 0)
    own_ref[...] = acc_ref[:edges, :]
    slots = rem_refs[0].shape[0]
    for j, rem_ref in enumerate(rem_refs):
        first = edges + j * slots
        rem_ref[...] = acc_ref[first : first + slots, :].astype(BF)


def fore_kernel(which_ref, down_ref, *rest):
    in_refs, (w_ref, k_ref, wbil_ref, bar_ref, cot_ref, out_ref, ext_ref, sum_ref, mask_ref) = (
        rest[:-9],
        rest[-9:],
    )
    basis, edges, width = sum_ref.shape
    trips = k_ref.shape[1]
    rows, cols = basis * GROUP, trips * GROUP
    table = ext_ref.shape[0]
    ext_ref[:edges, :] = down_ref[...]
    slots = in_refs[0].shape[0]
    for j, in_ref in enumerate(in_refs):
        first = edges + j * slots
        ext_ref[first : first + slots, :] = in_ref[...]
    mask_ref[...] = ones_where(iota((rows, cols), 0) % GROUP == iota((rows, cols), 1) % GROUP)
    spread = ones_where(iota((trips, cols), 0) == iota((trips, cols), 1) // GROUP)

    def body(g, carry):
        at = pl.ds(pl.multiple_of(g * GROUP, GROUP), GROUP)
        k = k_ref[at, :]
        lane = iota((GROUP, table), 1)
        pick = jnp.concatenate([ones_where(k[:, i : i + 1] == lane) for i in range(trips)], axis=0)
        got = dot(pick, ext_ref[...]).astype(BF)
        w = w_ref[:, at, :].reshape(rows, trips)
        diag = dot(w, spread).astype(BF) * mask_ref[...]
        sum_ref[:, at, :] = dot(diag, got).astype(BF).reshape(basis, GROUP, width)
        return carry

    lax.fori_loop(0, edges // GROUP, body, 0)
    agg = jnp.zeros((edges, width), F32)
    for b in range(0, basis, 2):
        pair = jnp.concatenate([sum_ref[b], sum_ref[b + 1]], axis=1)
        agg = agg + dot(pair, wbil_ref[b * width : (b + 2) * width, :])
    low = agg.astype(BF)
    span = out_ref.shape[0] // width - 2
    for h in range(2):
        part = dot(low, cot_ref[:, h * width : (h + 1) * width], TN)
        first = (span + h) * width
        out_ref[first : first + width, :] = part.astype(BF)
    bar = bar_ref[...]
    for j in range(span):
        part = dot(sum_ref[which_ref[0] * span + j], bar, TN)
        out_ref[j * width : (j + 1) * width, :] = part.astype(BF)


def last_kernel(own_ref, pre_ref, send_ref, wdown_ref, cot_ref, feats_ref, *rest):
    back_refs, (grad_ref, term_ref) = rest[:-2], rest[-2:]
    edges = own_ref.shape[0]
    slots = back_refs[0].shape[0]
    total = own_ref[...]
    for j, back_ref in enumerate(back_refs):
        place = ones_where(send_ref[:, j * slots : (j + 1) * slots] == iota((edges, slots), 0))
        total = total + dot(place, back_ref[...])
    pre_bar = (total * silu_grad(pre_ref[...].astype(F32))).astype(BF)
    grad_ref[...] = (cot_ref[...].astype(F32) + dot(pre_bar, wdown_ref[...], NT)).astype(BF)
    term_ref[...] = dot(feats_ref[...], pre_bar, TN).astype(BF)


def shifted(value, offset):
    count = lax.axis_size(DOM)
    return lax.ppermute(value, DOM, [(s, (s + offset) % count) for s in range(count)])


def scattered_sum(pieces, axis):
    arrived = lax.all_to_all(pieces, axis, 0, 0)
    return jnp.sum(arrived.astype(F32), axis=0).astype(BF)


def everywhere(value, axis):
    count = lax.axis_size(axis)
    copies = lax.optimization_barrier(jnp.broadcast_to(value[None], (count, *value.shape)))
    return lax.all_to_all(copies, axis, 0, 0)


def exchanged_sum(value, axis):
    return jnp.sum(everywhere(value, axis).astype(F32), axis=0).astype(BF)


def local(edge_feats, cotangent, w_down, w_up, w_bil, basis, trip_k, trip_count, send_rows):
    edges, span = edge_feats.shape
    width = w_down.shape[1]
    trips, basis_total, _ = basis.shape
    _, blocks, slots = send_rows.shape
    reach = blocks // 2
    offsets = [j + 1 if j < reach else reach - j - 1 for j in range(blocks)]
    feats = lax.axis_size("feat")
    groups = edges // GROUP
    low = lambda *shape: jax.ShapeDtypeStruct(shape, BF)

    part_pre = dot(edge_feats, w_down).astype(BF).reshape(feats, edges // feats, width)
    part_bar = dot(cotangent, w_up, NT).astype(BF).reshape(feats, edges // feats, width)
    both = scattered_sum(jnp.concatenate([part_pre, part_bar], axis=1), "feat")
    both = everywhere(both, "feat")
    pre = both[:, : edges // feats].reshape(edges, width)
    bar = both[:, edges // feats :].reshape(edges, width)

    live = jnp.arange(trips, dtype=jnp.int32)[:, None] < trip_count[None, :]
    weights = jnp.where(live[:, None, :], basis, 0.0).astype(BF)
    w_fore = weights.transpose(1, 2, 0)
    w_back = weights.transpose(0, 2, 1)
    k_rows = trip_k.T.reshape(trips, groups, GROUP).transpose(1, 0, 2).reshape(groups, 1, -1)

    down, *outgoing = call(
        down_kernel,
        [low(edges, width)] + [low(slots, width)] * blocks,
        [],
        2 * blocks * slots * edges * width,
        pre,
        send_rows.reshape(-1, 1),
    )
    incoming = [shifted(outgoing[j], offsets[j]) for j in range(blocks)]

    table = edges + blocks * slots
    big = 2 * edges * trips * width * (table + 3 * GROUP * basis_total)
    own, *remote = call(
        back_kernel,
        [jax.ShapeDtypeStruct((edges, width), F32)] + [low(slots, width)] * blocks,
        [
            pltpu.VMEM((basis_total, edges, width), BF),
            pltpu.VMEM((trips * GROUP, basis_total * GROUP), BF),
            pltpu.VMEM((table, width), F32),
        ],
        big,
        bar,
        w_bil,
        w_back,
        k_rows,
    )
    returned = [shifted(remote[j], -offsets[j]) for j in range(blocks)]

    own_rows = basis_total // feats * width
    which = lax.axis_index("feat").astype(jnp.int32).reshape(1)
    fore = functools.partial(
        pl.pallas_call,
        fore_kernel,
        in_specs=[pl.BlockSpec(memory_space=pltpu.SMEM)]
        + [pl.BlockSpec(memory_space=pltpu.VMEM)] * (blocks + 6),
        out_shape=low(own_rows + 2 * width, width),
        scratch_shapes=[
            pltpu.VMEM((table, width), BF),
            pltpu.VMEM((basis_total, edges, width), BF),
            pltpu.VMEM((basis_total * GROUP, trips * GROUP), BF),
        ],
        compiler_params=pltpu.CompilerParams(vmem_limit_bytes=40 << 20),
        cost_estimate=pl.CostEstimate(flops=big, bytes_accessed=8 << 20, transcendentals=0),
    )()
    early = fore(which, down, *incoming, w_fore, trip_k, w_bil, bar, cotangent)

    input_grad, late = call(
        last_kernel,
        [low(edges, span), low(span, width)],
        [],
        2 * edges * width * (blocks * slots + 2 * span),
        own,
        pre,
        send_rows.reshape(1, -1),
        w_down,
        cotangent,
        edge_feats,
        *returned,
    )

    near = ("y", "core")
    count = lax.axis_size(near)
    early = early.reshape(count, -1, width)
    late = late.reshape(count, -1, width)
    split = early.shape[1]
    total = scattered_sum(jnp.concatenate([early, late], axis=1), near)
    total = exchanged_sum(total, "zl")
    total = exchanged_sum(total, "zh")
    total = everywhere(total, near)
    factor = 1.0 / math.sqrt(edges * lax.axis_size(DOM))
    early = total[:, :split].reshape(-1, width).astype(F32) * factor
    late = total[:, split:].reshape(-1, width).astype(F32) * factor
    up = jnp.concatenate([early[own_rows : own_rows + width], early[own_rows + width :]], axis=1)
    return input_grad, late, up, early[:own_rows]


def solution(mesh):
    fine = Mesh(mesh.devices.reshape(4, 4, 4, 2, 4), (*DOM, "feat"))
    return jax.shard_map(
        local,
        mesh=fine,
        in_specs=(
            P(DOM, "feat"),
            P(DOM, "feat"),
            P("feat", None),
            P(None, "feat"),
            P(),
            P(None, None, DOM),
            P(DOM, None),
            P(DOM),
            P(DOM, None, None),
        ),
        out_specs=(P(DOM, "feat"), P("feat", None), P(None, "feat"), P("feat", None)),
        check_vma=False,
    )
```

```python
import math

import jax
import jax.numpy as jnp
from jax import lax
from jax.experimental import pallas as pl
from jax.experimental.pallas import tpu as pltpu
from jax.sharding import Mesh
from jax.sharding import PartitionSpec as P

BF = jnp.bfloat16
F32 = jnp.float32
NT = (((1,), (1,)), ((), ()))
TN = (((0,), (0,)), ((), ()))
DOM = ("zh", "zl", "y", "core")
LANES = 128
BACK_UNROLL = 8
FORE_UNROLL = 4
VMEM_BYTES = 40 << 20
GROUP = 16


def dot(a, b, dims=(((1,), (0,)), ((), ()))):
    return lax.dot_general(a, b, dims, preferred_element_type=F32)


def ones_where(cond):
    return jnp.where(cond, 1.0, 0.0).astype(BF)


def iota(shape, dim):
    return lax.broadcasted_iota(jnp.int32, shape, dim)


def silu_grad(value):
    sigma = jax.nn.sigmoid(value)
    return sigma * (1.0 + value * (1.0 - sigma))


def call(kernel, outs, scratch, flops, which, *args):
    moved_bytes = sum(a.size * a.dtype.itemsize for a in args)
    scalars = [pl.BlockSpec(memory_space=pltpu.SMEM)] if len(which) else []
    return pl.pallas_call(
        kernel,
        in_specs=scalars + [pl.BlockSpec(memory_space=pltpu.VMEM)] * len(args),
        out_shape=outs,
        scratch_shapes=scratch,
        compiler_params=pltpu.CompilerParams(vmem_limit_bytes=VMEM_BYTES),
        cost_estimate=pl.CostEstimate(flops=flops, bytes_accessed=moved_bytes, transcendentals=0),
    )(*([which] if len(which) else []), *args)


def down_kernel(pre_ref, send_ref, down_ref, *out_refs):
    pre = pre_ref[...].astype(F32)
    down = (pre * jax.nn.sigmoid(pre)).astype(BF)
    down_ref[...] = down
    slots = out_refs[0].shape[0]
    edges = down.shape[0]
    for j, out_ref in enumerate(out_refs):
        pick = ones_where(send_ref[j * slots : (j + 1) * slots, :] == iota((slots, edges), 1))
        out_ref[...] = dot(pick, down).astype(BF)


def chunks_swapped(tiles):
    tiles = list(tiles)
    chunk = iota(tiles[0].shape, 1) // GROUP
    for step in (4, 2, 1):
        low = (chunk & step) == 0
        for i in range(8):
            if i & step:
                continue
            a, b = tiles[i], tiles[i + step]
            tiles[i] = jnp.where(low, a, pltpu.roll(b, GROUP * step, 1))
            tiles[i + step] = jnp.where(low, pltpu.roll(a, LANES - GROUP * step, 1), b)
    return tiles


def prep_kernel(basis_ref, count_ref, by_basis_ref, by_trip_ref, live_ref):
    _, basis, _ = by_basis_ref.shape
    _, trips, _ = by_trip_ref.shape
    for t in range(count_ref.shape[1] // LANES):
        lanes = slice(t * LANES, (t + 1) * LANES)
        count = count_ref[:, lanes]
        tall = jnp.broadcast_to(count, (basis, LANES))
        for h in range(trips // 8):
            tiles = []
            for i in range(8 * h, 8 * h + 8):
                at = slice(i * basis, (i + 1) * basis)
                tiles.append(jnp.where(tall > i, basis_ref[at, lanes], 0.0))
                live_ref[at, :] = tiles[-1]
            for q, tile in enumerate(chunks_swapped(tiles)):
                by_basis_ref[8 * t + q, :, h * LANES : (h + 1) * LANES] = tile
        for o in range(basis // 8):
            octet = range(8 * o, 8 * o + 8)
            tiles = [live_ref[pl.ds(b, trips, stride=basis), :] for b in octet]
            for q, tile in enumerate(chunks_swapped(tiles)):
                by_trip_ref[8 * t + q, :, o * LANES : (o + 1) * LANES] = tile


def diagonal(rows):
    count, lanes = rows.shape
    same = iota((GROUP, lanes), 0) == iota((GROUP, lanes), 1) % GROUP
    parts = []
    for r in range(count):
        wide = jnp.broadcast_to(rows[r : r + 1, :], (GROUP, lanes))
        parts.append(jnp.where(same, wide, 0.0).astype(BF))
    return jnp.concatenate(parts, axis=0)


def back_kernel(which_ref, bar_ref, wbil_ref, w_ref, k_ref, own_ref, rem_a_ref, rem_b_ref, grad_ref, acc_ref):
    basis, edges, width = grad_ref.shape
    rows = k_ref.shape[2]
    slots = own_ref.shape[0]
    bar = bar_ref[...]
    for b in range(basis):
        grad_ref[b] = dot(bar, wbil_ref[b * width : (b + 1) * width, :], NT).astype(BF)
    acc_ref[...] = jnp.zeros_like(acc_ref)
    first = which_ref[0] * slots
    row = iota((3 * slots, rows), 0)
    block = row // slots
    jump = jnp.where(block == 0, 0, edges + (block - 1) * 4 * slots - block * slots)
    target = row + jump

    def body(g, carry):
        at = pl.ds(pl.multiple_of(g * GROUP, GROUP), GROUP)
        grad = grad_ref[:, at, :].reshape(basis * GROUP, width)
        d_rows = dot(diagonal(w_ref[g]), grad).astype(BF)
        pick = ones_where(k_ref[g] - first == target)
        acc_ref[...] += dot(pick, d_rows)
        return carry

    lax.fori_loop(0, edges // GROUP, body, 0, unroll=BACK_UNROLL)
    own_ref[...] = acc_ref[:slots, :].astype(BF)
    rem_a_ref[...] = acc_ref[slots : 2 * slots, :].astype(BF)
    rem_b_ref[...] = acc_ref[2 * slots :, :].astype(BF)


def fore_kernel(which_ref, down_ref, in_ref, w_ref, k_ref, wbil_ref, bar_ref, bil_ref, agg_ref, tab_ref, got_ref, sum_ref, all_ref):
    groups, rows, width = got_ref.shape
    basis = all_ref.shape[0]
    own, edges, _ = sum_ref.shape
    trips = k_ref.shape[1]
    tall = tab_ref.shape[0]
    highs = tab_ref.shape[1] // width
    slots = in_ref.shape[1] // 2
    parts = [down_ref[j * slots : (j + 1) * slots, :] for j in range(edges // slots)]
    parts += [in_ref[f, :slots, :] for f in range(4)] + [in_ref[f, slots:, :] for f in range(2)]
    per = tall // slots
    for j, part in enumerate(parts):
        h, p = j // per, j % per
        tab_ref[p * slots : (p + 1) * slots, h * width : (h + 1) * width] = part
    which = which_ref[0]

    def body(g, carry):
        at = pl.ds(pl.multiple_of(g * GROUP, GROUP), GROUP)
        k = k_ref[at, :]
        low, high = k & (tall - 1), k // tall
        lane = iota((GROUP, tall), 1)
        pick = jnp.concatenate([ones_where(low[:, i : i + 1] == lane) for i in range(trips)], axis=0)
        wide = dot(pick, tab_ref[...])
        kept = []
        for i in range(trips):
            part = wide[i * GROUP : (i + 1) * GROUP, :]
            mine = jnp.broadcast_to(high[:, i : i + 1], (GROUP, width))
            value = part[:, :width]
            for h in range(1, highs):
                value = jnp.where(mine == h, part[:, h * width : (h + 1) * width], value)
            kept.append(value.astype(BF))
        got = jnp.concatenate(kept, axis=0)
        got_ref[g] = got
        w = w_ref[g, pl.ds(pl.multiple_of(which * own, own), own), :]
        sum_ref[:, at, :] = dot(diagonal(w), got).astype(BF).reshape(own, GROUP, width)
        return carry

    lax.fori_loop(0, groups, body, 0, unroll=FORE_UNROLL)
    share = agg_ref.shape[0] // GROUP
    for q in range(share):
        g = which * share + q
        total = dot(diagonal(w_ref[g]), got_ref[g]).astype(BF)
        all_ref[:, q * GROUP : (q + 1) * GROUP, :] = total.reshape(basis, GROUP, width)
    agg = jnp.zeros(agg_ref.shape, F32)
    for b in range(0, basis, 2):
        pair = jnp.concatenate([all_ref[b], all_ref[b + 1]], axis=1)
        agg = agg + dot(pair, wbil_ref[b * width : (b + 2) * width, :])
    agg_ref[...] = agg.astype(BF)
    bar = bar_ref[...]
    for j in range(own):
        bil_ref[j * width : (j + 1) * width, :] = dot(sum_ref[j], bar, TN).astype(BF)


def last_kernel(got_ref, pre_ref, send_ref, wdown_ref, cot_ref, feats_ref, grad_ref, term_ref):
    edges, span = cot_ref.shape
    share = edges // got_ref.shape[0]
    width = got_ref.shape[2]
    feats = got_ref.shape[0]
    part = lambda j: [got_ref[f, j * share : (j + 1) * share, :] for f in range(feats)]
    blocks = part(1) + part(2)
    count = send_ref.shape[1] // share
    total = jnp.concatenate(part(0), axis=0).astype(F32)
    place = ones_where(send_ref[...] == iota((edges, count * share), 0))
    total = total + dot(place, jnp.concatenate(blocks[:count], axis=0))
    pre_bar = (total * silu_grad(pre_ref[...].astype(F32))).astype(BF)
    grad_ref[...] = (cot_ref[...].astype(F32) + dot(pre_bar, wdown_ref[...], NT)).astype(BF)
    term_ref[:span, :] = dot(feats_ref[...], pre_bar, TN).astype(BF)
    agg = jnp.concatenate(part(3), axis=0)
    for h in range(span // width):
        up = dot(agg, cot_ref[:, h * width : (h + 1) * width], TN)
        term_ref[span + h * width : span + (h + 1) * width, :] = up.astype(BF)


def moved(value, steps):
    domains, feats = lax.axis_size(DOM), lax.axis_size("feat")
    pairs = [
        (d * feats + f, (d + step) % domains * feats + f)
        for d in range(domains)
        for f, step in enumerate(steps[:feats])
        if step is not None
    ]
    return lax.ppermute(value, (*DOM, "feat"), pairs)


def scattered_sum(pieces, axis):
    arrived = lax.all_to_all(pieces, axis, 0, 0)
    return jnp.sum(arrived.astype(F32), axis=0).astype(BF)


def everywhere(value, axis):
    count = lax.axis_size(axis)
    copies = lax.optimization_barrier(jnp.broadcast_to(value[None], (count, *value.shape)))
    return lax.all_to_all(copies, axis, 0, 0)


def exchanged_sum(value, axis):
    return jnp.sum(everywhere(value, axis).astype(F32), axis=0).astype(BF)


def local(edge_feats, cotangent, w_down, w_up, w_bil, basis, trip_k, trip_count, send_rows):
    edges, span = edge_feats.shape
    width = w_down.shape[1]
    trips, basis_total, _ = basis.shape
    _, blocks, slots = send_rows.shape
    reach = blocks // 2
    offsets = [j + 1 if j < reach else reach - j - 1 for j in range(blocks)]
    feats = lax.axis_size("feat")
    groups = edges // GROUP
    own_basis = basis_total // feats
    low = lambda *shape: jax.ShapeDtypeStruct(shape, BF)
    feat = lax.axis_index("feat").astype(jnp.int32)
    which = feat.reshape(1)
    sends = offsets[:feats], (offsets[feats:] + [None] * feats)[:feats]
    backs = [[None if o is None else -o for o in steps] for steps in sends]

    part_pre = dot(edge_feats, w_down).astype(BF).reshape(feats, edges // feats, width)
    part_bar = dot(cotangent, w_up, NT).astype(BF).reshape(feats, edges // feats, width)
    both = scattered_sum(jnp.concatenate([part_pre, part_bar], axis=1), "feat")
    both = everywhere(both, "feat")
    pre = both[:, : edges // feats].reshape(edges, width)
    bar = both[:, edges // feats :].reshape(edges, width)

    by_basis, by_trip = call(
        prep_kernel,
        [
            jax.ShapeDtypeStruct((groups, basis_total, trips * GROUP), F32),
            jax.ShapeDtypeStruct((groups, trips, basis_total * GROUP), F32),
        ],
        [pltpu.VMEM((trips * basis_total, LANES), F32)],
        1 << 28,
        (),
        basis.reshape(trips * basis_total, edges),
        trip_count.reshape(1, edges),
    )
    k_rows = trip_k.T.reshape(trips, groups, GROUP).transpose(1, 0, 2).reshape(groups, 1, -1)

    second = jnp.minimum(feats + feat, blocks - 1)
    listed = jnp.concatenate([send_rows[0, feat], send_rows[0, second]]).reshape(-1, 1)
    down, out_a, out_b = call(
        down_kernel,
        [low(edges, width), low(slots, width), low(slots, width)],
        [],
        4 * slots * edges * width,
        (),
        pre,
        listed,
    )
    in_a, in_b = moved(out_a, sends[0]), moved(out_b, sends[1])

    table = edges + blocks * slots
    big = 2 * edges * trips * width * 2000
    own, rem_a, rem_b = call(
        back_kernel,
        [low(slots, width)] * 3,
        [
            pltpu.VMEM((basis_total, edges, width), BF),
            pltpu.VMEM((3 * slots, width), F32),
        ],
        big,
        which,
        bar,
        w_bil,
        by_trip,
        k_rows,
    )
    back_a, back_b = moved(rem_a, backs[0]), moved(rem_b, backs[1])

    incoming, own = lax.optimization_barrier((jnp.concatenate([in_a, in_b], axis=0), own))
    incoming = everywhere(incoming, "feat")
    tall = 2 * slots
    bil, agg = call(
        fore_kernel,
        [low(own_basis * width, width), low(edges // feats, width)],
        [
            pltpu.VMEM((tall, table // tall * width), BF),
            pltpu.VMEM((groups, trips * GROUP, width), BF),
            pltpu.VMEM((own_basis, edges, width), BF),
            pltpu.VMEM((basis_total, edges // feats, width), BF),
        ],
        big,
        which,
        down,
        incoming,
        by_basis,
        trip_k,
        w_bil,
        bar,
    )
    shared = everywhere(jnp.concatenate([own, back_a, back_b, agg], axis=0), "feat")
    input_grad, terms = call(
        last_kernel,
        [low(edges, span), low(2 * span, width)],
        [],
        2 * edges * width * (blocks * slots + 3 * span),
        (),
        shared,
        pre,
        send_rows.reshape(1, -1),
        w_down,
        cotangent,
        edge_feats,
    )

    near = ("y", "core")
    count = lax.axis_size(near)
    bil = bil.reshape(count, -1, width)
    terms = terms.reshape(count, -1, width)
    split = bil.shape[1]
    total = scattered_sum(jnp.concatenate([bil, terms], axis=1), near)
    total = exchanged_sum(total, "zl")
    total = exchanged_sum(total, "zh")
    total = everywhere(total, near)
    factor = 1.0 / math.sqrt(edges * lax.axis_size(DOM))
    bil = total[:, :split].reshape(-1, width).astype(F32) * factor
    terms = total[:, split:].reshape(-1, width).astype(F32) * factor
    up = jnp.concatenate([terms[span : span + width], terms[span + width :]], axis=1)
    return input_grad, terms[:span], up, bil


def solution(mesh):
    fine = Mesh(mesh.devices.reshape(4, 4, 4, 2, 4), (*DOM, "feat"))
    return jax.shard_map(
        local,
        mesh=fine,
        in_specs=(
            P(DOM, "feat"),
            P(DOM, "feat"),
            P("feat", None),
            P(None, "feat"),
            P(),
            P(None, None, DOM),
            P(DOM, None),
            P(DOM),
            P(DOM, None, None),
        ),
        out_specs=(P(DOM, "feat"), P("feat", None), P(None, "feat"), P("feat", None)),
        check_vma=False,
    )
```

```python
import functools
import math

import jax
import jax.numpy as jnp
from jax import lax
from jax.experimental import pallas as pl
from jax.experimental.pallas import tpu as pltpu
from jax.sharding import Mesh
from jax.sharding import PartitionSpec as P

BF = jnp.bfloat16
F32 = jnp.float32
NT = (((1,), (1,)), ((), ()))
TN = (((0,), (0,)), ((), ()))
DOM = ("zh", "zl", "y", "core")
LANES = 128
BACK_UNROLL = 8
GATHER_UNROLL = 2
SUM_UNROLL = 4
PAIR = 4
VMEM_BYTES = 20 << 20
GROUP = 16


def dot(a, b, dims=(((1,), (0,)), ((), ()))):
    return lax.dot_general(a, b, dims, preferred_element_type=F32)


def ones_where(cond):
    return jnp.where(cond, 1.0, 0.0).astype(BF)


def iota(shape, dim):
    return lax.broadcasted_iota(jnp.int32, shape, dim)


def silu_grad(value):
    sigma = jax.nn.sigmoid(value)
    return sigma * (1.0 + value * (1.0 - sigma))


def call(kernel, outs, scratch, flops, which, *args, late=()):
    moved_bytes = sum(a.size * a.dtype.itemsize for a in args)
    scalars = [pl.BlockSpec(memory_space=pltpu.SMEM)] if len(which) else []
    return pl.pallas_call(
        kernel,
        in_specs=scalars
        + [pl.BlockSpec(memory_space=pltpu.VMEM)] * len(args)
        + [pl.BlockSpec(memory_space=pltpu.HBM)] * len(late),
        out_shape=outs,
        scratch_shapes=scratch
        + [pltpu.VMEM(a.shape, a.dtype) for a in late]
        + [pltpu.SemaphoreType.DMA] * len(late),
        compiler_params=pltpu.CompilerParams(vmem_limit_bytes=VMEM_BYTES),
        cost_estimate=pl.CostEstimate(flops=flops, bytes_accessed=moved_bytes, transcendentals=0),
    )(*([which] if len(which) else []), *args, *(pltpu.with_memory_space_constraint(a, pltpu.HBM) for a in late))


def down_kernel(both_ref, send_ref, pre_ref, bar_ref, down_ref, *out_refs):
    edges = pre_ref.shape[0]
    pre, bar = both_ref[0, :edges, :].astype(F32), both_ref[0, edges:, :].astype(F32)
    for f in range(1, both_ref.shape[0]):
        pre = pre + both_ref[f, :edges, :].astype(F32)
        bar = bar + both_ref[f, edges:, :].astype(F32)
    pre_ref[...] = pre
    bar_ref[...] = bar.astype(BF)
    down = (pre * jax.nn.sigmoid(pre)).astype(BF)
    down_ref[...] = down
    slots = out_refs[0].shape[0]
    for j, out_ref in enumerate(out_refs):
        pick = ones_where(send_ref[j * slots : (j + 1) * slots, :] == iota((slots, edges), 1))
        out_ref[...] = dot(pick, down).astype(BF)


def chunks_swapped(tiles):
    tiles = list(tiles)
    chunk = iota(tiles[0].shape, 1) // GROUP
    for step in (4, 2, 1):
        low = (chunk & step) == 0
        for i in range(8):
            if i & step:
                continue
            a, b = tiles[i], tiles[i + step]
            tiles[i] = jnp.where(low, a, pltpu.roll(b, GROUP * step, 1))
            tiles[i + step] = jnp.where(low, pltpu.roll(a, LANES - GROUP * step, 1), b)
    return tiles


def prep_kernel(basis_ref, count_ref, by_basis_ref, by_trip_ref, live_ref):
    _, basis, _ = by_basis_ref.shape
    _, trips, _ = by_trip_ref.shape
    for t in range(count_ref.shape[1] // LANES):
        lanes = slice(t * LANES, (t + 1) * LANES)
        count = count_ref[:, lanes]
        tall = jnp.broadcast_to(count, (basis, LANES))
        for h in range(trips // 8):
            tiles = []
            for i in range(8 * h, 8 * h + 8):
                at = slice(i * basis, (i + 1) * basis)
                tiles.append(jnp.where(tall > i, basis_ref[at, lanes], 0.0))
                live_ref[at, :] = tiles[-1]
            for q, tile in enumerate(chunks_swapped(tiles)):
                by_basis_ref[8 * t + q, :, h * LANES : (h + 1) * LANES] = tile
        for o in range(basis // 8):
            octet = range(8 * o, 8 * o + 8)
            tiles = [live_ref[pl.ds(b, trips, stride=basis), :] for b in octet]
            for q, tile in enumerate(chunks_swapped(tiles)):
                by_trip_ref[8 * t + q, :, o * LANES : (o + 1) * LANES] = tile


def diagonal(rows):
    count, lanes = rows.shape
    same = iota((GROUP, lanes), 0) == iota((GROUP, lanes), 1) % GROUP
    parts = []
    for r in range(count):
        wide = jnp.broadcast_to(rows[r : r + 1, :], (GROUP, lanes))
        parts.append(jnp.where(same, wide, 0.0).astype(BF))
    return jnp.concatenate(parts, axis=0)


def back_kernel(
    which_ref,
    bar_ref,
    k_ref,
    w_far,
    wbil_far,
    own_ref,
    rem_a_ref,
    rem_b_ref,
    grad_ref,
    acc_ref,
    part_sems,
    w_ref,
    wbil_ref,
    w_sem,
    _,
):
    basis, edges, width = grad_ref.shape
    rows = k_ref.shape[2]
    slots = own_ref.shape[0]
    fetch = pltpu.make_async_copy(w_far, w_ref, w_sem)
    parts = part_sems.shape[0]
    some = wbil_ref.shape[0] // parts
    fetch_parts = []
    for p in range(parts):
        at = pl.ds(p * some, some)
        fetch_parts.append(pltpu.make_async_copy(wbil_far.at[at], wbil_ref.at[at], part_sems.at[p]))
        fetch_parts[p].start()
    fetch.start()
    bar = bar_ref[...]
    for b in range(basis):
        if b % (basis // parts) == 0:
            fetch_parts[b // (basis // parts)].wait()
        grad_ref[b] = dot(bar, wbil_ref[b * width : (b + 1) * width, :], NT).astype(BF)
    acc_ref[...] = jnp.zeros_like(acc_ref)
    first = which_ref[0] * slots
    row = iota((3 * slots, rows), 0)
    block = row // slots
    jump = jnp.where(block == 0, 0, edges + (block - 1) * 4 * slots - block * slots)
    target = row + jump
    fetch.wait()

    def body(g, carry):
        at = pl.ds(pl.multiple_of(g * GROUP, GROUP), GROUP)
        grad = grad_ref[:, at, :].reshape(basis * GROUP, width)
        d_rows = dot(diagonal(w_ref[g]), grad).astype(BF)
        k = jnp.broadcast_to(k_ref[g] - first, target.shape).astype(jnp.int16)
        pick = jnp.where(k == target.astype(jnp.int16), jnp.ones((), BF), jnp.zeros((), BF))
        acc_ref[...] += dot(pick, d_rows)
        return carry

    lax.fori_loop(0, edges // GROUP, body, 0, unroll=BACK_UNROLL)
    own_ref[...] = acc_ref[:slots, :].astype(BF)
    rem_a_ref[...] = acc_ref[slots : 2 * slots, :].astype(BF)
    rem_b_ref[...] = acc_ref[2 * slots :, :].astype(BF)


def fore_kernel(
    which_ref,
    down_ref,
    in_ref,
    k_ref,
    bar_ref,
    w_far,
    wbil_far,
    cot_far,
    term_ref,
    tab_ref,
    got_ref,
    sum_ref,
    w_ref,
    wbil_ref,
    cot_ref,
    w_sem,
    wbil_sem,
    cot_sem,
):
    fetch_w = pltpu.make_async_copy(w_far, w_ref, w_sem)
    fetch_wbil = pltpu.make_async_copy(wbil_far, wbil_ref, wbil_sem)
    fetch_cot = pltpu.make_async_copy(cot_far, cot_ref, cot_sem)
    fetch_w.start()
    fetch_wbil.start()
    fetch_cot.start()
    groups, rows, width = got_ref.shape
    basis, edges, _ = sum_ref.shape
    trips = k_ref.shape[1]
    tall = tab_ref.shape[0]
    highs = tab_ref.shape[1] // width
    slots = in_ref.shape[1] // 2
    parts = [down_ref[j * slots : (j + 1) * slots, :] for j in range(edges // slots)]
    parts += [in_ref[f, :slots, :] for f in range(4)] + [in_ref[f, slots:, :] for f in range(2)]
    highs, tall = 1, tab_ref.shape[0]
    for j, part in enumerate(parts):
        tab_ref[j * slots : (j + 1) * slots, :] = part

    def gather(n, carry):
        lane = iota((GROUP, tall * highs), 1).astype(jnp.int16)
        for j in range(PAIR):
            g = n * PAIR + j
            at = pl.ds(pl.multiple_of(g * GROUP, GROUP), GROUP)
            k = k_ref[at, :].astype(jnp.int16)
            picks = [
                jnp.where(k[:, i : i + 1] == lane, jnp.ones((), BF), jnp.zeros((), BF))
                for i in range(trips)
            ]
            got_ref[g] = dot(jnp.concatenate(picks, axis=0), tab_ref[...]).astype(BF)
        return carry

    lax.fori_loop(0, groups // PAIR, gather, 0, unroll=GATHER_UNROLL)

    fetch_w.wait()

    def add_up(g, carry):
        at = pl.ds(pl.multiple_of(g * GROUP, GROUP), GROUP)
        total = dot(diagonal(w_ref[g]), got_ref[g]).astype(BF)
        sum_ref[:, at, :] = total.reshape(basis, GROUP, width)
        return carry

    lax.fori_loop(0, groups, add_up, 0, unroll=SUM_UNROLL)
    fetch_wbil.wait()
    fetch_cot.wait()
    agg = jnp.zeros((edges, width), F32)
    for b in range(0, basis, 2):
        pair = jnp.concatenate([sum_ref[b], sum_ref[b + 1]], axis=1)
        agg = agg + dot(pair, wbil_ref[b * width : (b + 2) * width, :])
    agg = agg.astype(BF)
    bar = bar_ref[...]
    own = term_ref.shape[0] // width - cot_ref.shape[1] // width
    for j in range(own):
        part = dot(sum_ref[which_ref[0] * own + j], bar, TN)
        term_ref[j * width : (j + 1) * width, :] = part.astype(BF)
    for h in range(cot_ref.shape[1] // width):
        up = dot(agg, cot_ref[:, h * width : (h + 1) * width], TN)
        term_ref[(own + h) * width : (own + h + 1) * width, :] = up.astype(BF)


def last_kernel(got_ref, pre_ref, send_ref, wdown_ref, cot_ref, feats_ref, grad_ref, term_ref):
    edges, span = cot_ref.shape
    share = edges // got_ref.shape[0]
    feats = got_ref.shape[0]
    part = lambda j: [got_ref[f, j * share : (j + 1) * share, :] for f in range(feats)]
    blocks = part(1) + part(2)
    count = send_ref.shape[1] // share
    total = jnp.concatenate(part(0), axis=0).astype(F32)
    place = ones_where(send_ref[...] == iota((edges, count * share), 0))
    total = total + dot(place, jnp.concatenate(blocks[:count], axis=0))
    pre_bar = (total * silu_grad(pre_ref[...])).astype(BF)
    grad_ref[...] = (cot_ref[...].astype(F32) + dot(pre_bar, wdown_ref[...], NT)).astype(BF)
    term_ref[...] = dot(feats_ref[...], pre_bar, TN).astype(BF)


def out_kernel(factor, total_ref, down_ref, up_ref, bil_ref):
    pieces, rows, width = total_ref.shape
    late = down_ref.shape[0] // pieces
    early = rows - late
    full = total_ref[...].astype(F32) * factor
    down_ref[...] = full[:, early:, :].reshape(down_ref.shape)
    flat = full[:, :early, :].reshape(pieces * early, width)
    own = bil_ref.shape[0]
    bil_ref[...] = flat[:own, :]
    for h in range(up_ref.shape[1] // width):
        up_ref[:, h * width : (h + 1) * width] = flat[own + h * width : own + (h + 1) * width, :]


def moved(value, steps):
    domains, feats = lax.axis_size(DOM), lax.axis_size("feat")
    pairs = [
        (d * feats + f, (d + step) % domains * feats + f)
        for d in range(domains)
        for f, step in enumerate(steps[:feats])
        if step is not None
    ]
    return lax.ppermute(value, (*DOM, "feat"), pairs)


def scattered_sum(pieces, axis):
    arrived = lax.all_to_all(pieces, axis, 0, 0)
    return jnp.sum(arrived.astype(F32), axis=0).astype(BF)


def everywhere(value, axis):
    count = lax.axis_size(axis)
    copies = lax.optimization_barrier(jnp.broadcast_to(value[None], (count, *value.shape)))
    return lax.all_to_all(copies, axis, 0, 0)


def exchanged_sum(value, axis):
    return jnp.sum(everywhere(value, axis).astype(F32), axis=0).astype(BF)


def local(edge_feats, cotangent, w_down, w_up, w_bil, basis, trip_k, trip_count, send_rows):
    edges, span = edge_feats.shape
    width = w_down.shape[1]
    trips, basis_total, _ = basis.shape
    _, blocks, slots = send_rows.shape
    reach = blocks // 2
    offsets = [j + 1 if j < reach else reach - j - 1 for j in range(blocks)]
    feats = lax.axis_size("feat")
    groups = edges // GROUP
    own_basis = basis_total // feats
    low = lambda *shape: jax.ShapeDtypeStruct(shape, BF)
    feat = lax.axis_index("feat").astype(jnp.int32)
    which = feat.reshape(1)
    sends = offsets[:feats], (offsets[feats:] + [None] * feats)[:feats]
    backs = [[None if o is None else -o for o in steps] for steps in sends]

    part_pre = dot(edge_feats, w_down).astype(BF)
    part_bar = dot(cotangent, w_up, NT).astype(BF)
    both = everywhere(jnp.concatenate([part_pre, part_bar], axis=0), "feat")

    by_basis, by_trip = call(
        prep_kernel,
        [
            jax.ShapeDtypeStruct((groups, basis_total, trips * GROUP), F32),
            jax.ShapeDtypeStruct((groups, trips, basis_total * GROUP), F32),
        ],
        [pltpu.VMEM((trips * basis_total, LANES), F32)],
        1 << 28,
        (),
        basis.reshape(trips * basis_total, edges),
        trip_count.reshape(1, edges),
    )
    k_rows = trip_k.T.reshape(trips, groups, GROUP).transpose(1, 0, 2).reshape(groups, 1, -1)

    second = jnp.minimum(feats + feat, blocks - 1)
    listed = jnp.concatenate([send_rows[0, feat], send_rows[0, second]]).reshape(-1, 1)
    pre, bar, down, out_a, out_b = call(
        down_kernel,
        [jax.ShapeDtypeStruct((edges, width), F32)]
        + [low(edges, width)] * 2
        + [low(slots, width)] * 2,
        [],
        4 * slots * edges * width,
        (),
        both,
        listed,
    )
    in_a, in_b = moved(out_a, sends[0]), moved(out_b, sends[1])

    table = edges + blocks * slots
    big = 2 * edges * trips * width * 2000
    own, rem_a, rem_b = call(
        back_kernel,
        [low(slots, width)] * 3,
        [
            pltpu.VMEM((basis_total, edges, width), BF),
            pltpu.VMEM((3 * slots, width), F32),
            pltpu.SemaphoreType.DMA((4,)),
        ],
        big,
        which,
        bar,
        k_rows,
        late=(by_trip, w_bil),
    )
    back_a, back_b = moved(rem_a, backs[0]), moved(rem_b, backs[1])

    incoming, own = lax.optimization_barrier((jnp.concatenate([in_a, in_b], axis=0), own))
    incoming = everywhere(incoming, "feat")
    tall = 2 * slots
    shared = everywhere(jnp.concatenate([own, back_a, back_b], axis=0), "feat")
    early = call(
        fore_kernel,
        low(own_basis * width + span, width),
        [
            pltpu.VMEM((table, width), BF),
            pltpu.VMEM((groups, trips * GROUP, width), BF),
            pltpu.VMEM((basis_total, edges, width), BF),
        ],
        big,
        which,
        down,
        incoming,
        trip_k,
        bar,
        late=(by_basis, w_bil, cotangent),
    )
    input_grad, late = call(
        last_kernel,
        [low(edges, span), low(span, width)],
        [],
        2 * edges * width * (blocks * slots + 3 * span),
        (),
        shared,
        pre,
        send_rows.reshape(1, -1),
        w_down,
        cotangent,
        edge_feats,
    )

    near = ("y", "core")
    count = lax.axis_size(near)
    pieces = [early.reshape(count, -1, width), late.reshape(count, -1, width)]
    total = scattered_sum(jnp.concatenate(pieces, axis=1), near)
    total = exchanged_sum(total, "zl")
    total = exchanged_sum(total, "zh")
    total = everywhere(total, near)
    factor = 1.0 / math.sqrt(edges * lax.axis_size(DOM))
    down_grad, up_grad, bil_grad = call(
        functools.partial(out_kernel, factor),
        [
            jax.ShapeDtypeStruct((span, width), F32),
            jax.ShapeDtypeStruct((width, span), F32),
            jax.ShapeDtypeStruct((own_basis * width, width), F32),
        ],
        [],
        1 << 20,
        (),
        total,
    )
    return input_grad, down_grad, up_grad, bil_grad


def solution(mesh):
    fine = Mesh(mesh.devices.reshape(4, 4, 4, 2, 4), (*DOM, "feat"))
    return jax.shard_map(
        local,
        mesh=fine,
        in_specs=(
            P(DOM, "feat"),
            P(DOM, "feat"),
            P("feat", None),
            P(None, "feat"),
            P(),
            P(None, None, DOM),
            P(DOM, None),
            P(DOM),
            P(DOM, None, None),
        ),
        out_specs=(P(DOM, "feat"), P("feat", None), P(None, "feat"), P("feat", None)),
        check_vma=False,
    )
```

```python
import functools
import math

import jax
import jax.numpy as jnp
from jax import lax
from jax.experimental import pallas as pl
from jax.experimental.pallas import tpu as pltpu
from jax.sharding import Mesh
from jax.sharding import PartitionSpec as P

BF = jnp.bfloat16
F32 = jnp.float32
NT = (((1,), (1,)), ((), ()))
TN = (((0,), (0,)), ((), ()))
DOM = ("zh", "zl", "y", "core")
LANES = 128
BACK_UNROLL = 8
GATHER_UNROLL = 2
SUM_UNROLL = 4
PAIR = 4
VMEM_BYTES = 20 << 20
GROUP = 16


def dot(a, b, dims=(((1,), (0,)), ((), ()))):
    return lax.dot_general(a, b, dims, preferred_element_type=F32)


def ones_where(cond):
    return jnp.where(cond, 1.0, 0.0).astype(BF)


def iota(shape, dim):
    return lax.broadcasted_iota(jnp.int32, shape, dim)


def silu_grad(value):
    sigma = jax.nn.sigmoid(value)
    return sigma * (1.0 + value * (1.0 - sigma))


def call(kernel, outs, scratch, flops, which, *args, late=()):
    moved_bytes = sum(a.size * a.dtype.itemsize for a in args)
    scalars = [pl.BlockSpec(memory_space=pltpu.SMEM)] if len(which) else []
    return pl.pallas_call(
        kernel,
        in_specs=scalars
        + [pl.BlockSpec(memory_space=pltpu.VMEM)] * len(args)
        + [pl.BlockSpec(memory_space=pltpu.HBM)] * len(late),
        out_shape=outs,
        scratch_shapes=scratch
        + [pltpu.VMEM(a.shape, a.dtype) for a in late]
        + [pltpu.SemaphoreType.DMA] * len(late),
        compiler_params=pltpu.CompilerParams(vmem_limit_bytes=VMEM_BYTES),
        cost_estimate=pl.CostEstimate(flops=flops, bytes_accessed=moved_bytes, transcendentals=0),
    )(*([which] if len(which) else []), *args, *(pltpu.with_memory_space_constraint(a, pltpu.HBM) for a in late))


def down_kernel(both_ref, send_ref, pre_ref, bar_ref, down_ref, *out_refs):
    edges = pre_ref.shape[0]
    pre, bar = both_ref[0, :edges, :].astype(F32), both_ref[0, edges:, :].astype(F32)
    for f in range(1, both_ref.shape[0]):
        pre = pre + both_ref[f, :edges, :].astype(F32)
        bar = bar + both_ref[f, edges:, :].astype(F32)
    pre_ref[...] = pre
    bar_ref[...] = bar.astype(BF)
    down = (pre * jax.nn.sigmoid(pre)).astype(BF)
    down_ref[...] = down
    slots = out_refs[0].shape[0]
    for j, out_ref in enumerate(out_refs):
        pick = ones_where(send_ref[j * slots : (j + 1) * slots, :] == iota((slots, edges), 1))
        out_ref[...] = dot(pick, down).astype(BF)


def chunks_swapped(tiles):
    tiles = list(tiles)
    chunk = iota(tiles[0].shape, 1) // GROUP
    for step in (4, 2, 1):
        low = (chunk & step) == 0
        for i in range(8):
            if i & step:
                continue
            a, b = tiles[i], tiles[i + step]
            tiles[i] = jnp.where(low, a, pltpu.roll(b, GROUP * step, 1))
            tiles[i + step] = jnp.where(low, pltpu.roll(a, LANES - GROUP * step, 1), b)
    return tiles


def prep_kernel(basis_ref, count_ref, by_basis_ref, by_trip_ref, live_ref):
    _, basis, _ = by_basis_ref.shape
    _, trips, _ = by_trip_ref.shape
    for t in range(count_ref.shape[1] // LANES):
        lanes = slice(t * LANES, (t + 1) * LANES)
        count = count_ref[:, lanes]
        tall = jnp.broadcast_to(count, (basis, LANES))
        for h in range(trips // 8):
            tiles = []
            for i in range(8 * h, 8 * h + 8):
                at = slice(i * basis, (i + 1) * basis)
                tiles.append(jnp.where(tall > i, basis_ref[at, lanes], 0.0))
                live_ref[at, :] = tiles[-1]
            for q, tile in enumerate(chunks_swapped(tiles)):
                by_basis_ref[8 * t + q, :, h * LANES : (h + 1) * LANES] = tile
        for o in range(basis // 8):
            octet = range(8 * o, 8 * o + 8)
            tiles = [live_ref[pl.ds(b, trips, stride=basis), :] for b in octet]
            for q, tile in enumerate(chunks_swapped(tiles)):
                by_trip_ref[8 * t + q, :, o * LANES : (o + 1) * LANES] = tile


def diagonal(rows):
    count, lanes = rows.shape
    same = iota((GROUP, lanes), 0) == iota((GROUP, lanes), 1) % GROUP
    parts = []
    for r in range(count):
        wide = jnp.broadcast_to(rows[r : r + 1, :], (GROUP, lanes))
        parts.append(jnp.where(same, wide, 0.0).astype(BF))
    return jnp.concatenate(parts, axis=0)


def back_kernel(
    which_ref,
    bar_ref,
    k_ref,
    w_far,
    wbil_far,
    own_ref,
    rem_a_ref,
    rem_b_ref,
    grad_ref,
    acc_ref,
    part_sems,
    w_ref,
    wbil_ref,
    w_sem,
    _,
):
    basis, edges, width = grad_ref.shape
    rows = k_ref.shape[2]
    slots = own_ref.shape[0]
    fetch = pltpu.make_async_copy(w_far, w_ref, w_sem)
    parts = part_sems.shape[0]
    some = wbil_ref.shape[0] // parts
    fetch_parts = []
    for p in range(parts):
        at = pl.ds(p * some, some)
        fetch_parts.append(pltpu.make_async_copy(wbil_far.at[at], wbil_ref.at[at], part_sems.at[p]))
        fetch_parts[p].start()
    fetch.start()
    bar = bar_ref[...]
    for b in range(basis):
        if b % (basis // parts) == 0:
            fetch_parts[b // (basis // parts)].wait()
        grad_ref[b] = dot(bar, wbil_ref[b * width : (b + 1) * width, :], NT).astype(BF)
    acc_ref[...] = jnp.zeros_like(acc_ref)
    first = which_ref[0] * slots
    row = iota((3 * slots, rows), 0)
    block = row // slots
    jump = jnp.where(block == 0, 0, edges + (block - 1) * 4 * slots - block * slots)
    target = row + jump
    fetch.wait()

    def body(g, carry):
        at = pl.ds(pl.multiple_of(g * GROUP, GROUP), GROUP)
        grad = grad_ref[:, at, :].reshape(basis * GROUP, width)
        d_rows = dot(diagonal(w_ref[g]), grad).astype(BF)
        k = jnp.broadcast_to(k_ref[g] - first, target.shape).astype(jnp.int16)
        pick = jnp.where(k == target.astype(jnp.int16), jnp.ones((), BF), jnp.zeros((), BF))
        acc_ref[...] += dot(pick, d_rows)
        return carry

    lax.fori_loop(0, edges // GROUP, body, 0, unroll=BACK_UNROLL)
    own_ref[...] = acc_ref[:slots, :].astype(BF)
    rem_a_ref[...] = acc_ref[slots : 2 * slots, :].astype(BF)
    rem_b_ref[...] = acc_ref[2 * slots :, :].astype(BF)


def fore_kernel(
    which_ref,
    down_ref,
    in_ref,
    k_ref,
    bar_ref,
    w_far,
    wbil_far,
    cot_far,
    term_ref,
    tab_ref,
    got_ref,
    sum_ref,
    w_ref,
    wbil_ref,
    cot_ref,
    w_sem,
    wbil_sem,
    cot_sem,
):
    fetch_w = pltpu.make_async_copy(w_far, w_ref, w_sem)
    fetch_wbil = pltpu.make_async_copy(wbil_far, wbil_ref, wbil_sem)
    fetch_cot = pltpu.make_async_copy(cot_far, cot_ref, cot_sem)
    fetch_w.start()
    fetch_wbil.start()
    fetch_cot.start()
    groups, _, width = got_ref.shape
    basis, edges, _ = sum_ref.shape
    trips = k_ref.shape[1]
    tall = tab_ref.shape[0]
    highs = tab_ref.shape[1] // width
    slots = in_ref.shape[1] // 2
    parts = [down_ref[j * slots : (j + 1) * slots, :] for j in range(edges // slots)]
    parts += [in_ref[f, :slots, :] for f in range(4)] + [in_ref[f, slots:, :] for f in range(2)]
    highs, tall = 1, tab_ref.shape[0]
    for j, part in enumerate(parts):
        tab_ref[j * slots : (j + 1) * slots, :] = part

    def gather(n, carry):
        lane = iota((GROUP, tall * highs), 1).astype(jnp.int16)
        for j in range(PAIR):
            g = n * PAIR + j
            at = pl.ds(pl.multiple_of(g * GROUP, GROUP), GROUP)
            k = k_ref[at, :].astype(jnp.int16)
            picks = [
                jnp.where(k[:, i : i + 1] == lane, jnp.ones((), BF), jnp.zeros((), BF))
                for i in range(trips)
            ]
            got_ref[g] = dot(jnp.concatenate(picks, axis=0), tab_ref[...]).astype(BF)
        return carry

    lax.fori_loop(0, groups // PAIR, gather, 0, unroll=GATHER_UNROLL)

    fetch_w.wait()

    def add_up(g, carry):
        at = pl.ds(pl.multiple_of(g * GROUP, GROUP), GROUP)
        total = dot(diagonal(w_ref[g]), got_ref[g]).astype(BF)
        sum_ref[:, at, :] = total.reshape(basis, GROUP, width)
        return carry

    lax.fori_loop(0, groups, add_up, 0, unroll=SUM_UNROLL)
    fetch_wbil.wait()
    fetch_cot.wait()
    agg = jnp.zeros((edges, width), F32)
    for b in range(0, basis, 2):
        pair = jnp.concatenate([sum_ref[b], sum_ref[b + 1]], axis=1)
        agg = agg + dot(pair, wbil_ref[b * width : (b + 2) * width, :])
    agg = agg.astype(BF)
    bar = bar_ref[...]
    own = term_ref.shape[0] // width - cot_ref.shape[1] // width
    for j in range(own):
        part = dot(sum_ref[which_ref[0] * own + j], bar, TN)
        term_ref[j * width : (j + 1) * width, :] = part.astype(BF)
    for h in range(cot_ref.shape[1] // width):
        up = dot(agg, cot_ref[:, h * width : (h + 1) * width], TN)
        term_ref[(own + h) * width : (own + h + 1) * width, :] = up.astype(BF)


def last_kernel(got_ref, pre_ref, send_ref, wdown_ref, cot_ref, feats_ref, grad_ref, term_ref):
    edges, _ = cot_ref.shape
    share = edges // got_ref.shape[0]
    feats = got_ref.shape[0]
    part = lambda j: [got_ref[f, j * share : (j + 1) * share, :] for f in range(feats)]
    blocks = part(1) + part(2)
    count = send_ref.shape[1] // share
    total = jnp.concatenate(part(0), axis=0).astype(F32)
    place = ones_where(send_ref[...] == iota((edges, count * share), 0))
    total = total + dot(place, jnp.concatenate(blocks[:count], axis=0))
    pre_bar = (total * silu_grad(pre_ref[...])).astype(BF)
    grad_ref[...] = (cot_ref[...].astype(F32) + dot(pre_bar, wdown_ref[...], NT)).astype(BF)
    term_ref[...] = dot(feats_ref[...], pre_bar, TN).astype(BF)


def out_kernel(factor, total_ref, down_ref, up_ref, bil_ref):
    pieces, rows, width = total_ref.shape
    late = down_ref.shape[0] // pieces
    early = rows - late
    full = total_ref[...].astype(F32) * factor
    down_ref[...] = full[:, early:, :].reshape(down_ref.shape)
    flat = full[:, :early, :].reshape(pieces * early, width)
    own = bil_ref.shape[0]
    bil_ref[...] = flat[:own, :]
    for h in range(up_ref.shape[1] // width):
        up_ref[:, h * width : (h + 1) * width] = flat[own + h * width : own + (h + 1) * width, :]


def moved(value, steps):
    domains, feats = lax.axis_size(DOM), lax.axis_size("feat")
    pairs = [
        (d * feats + f, (d + step) % domains * feats + f)
        for d in range(domains)
        for f, step in enumerate(steps[:feats])
        if step is not None
    ]
    return lax.ppermute(value, (*DOM, "feat"), pairs)


def scattered_sum(pieces, axis):
    arrived = lax.all_to_all(pieces, axis, 0, 0)
    return jnp.sum(arrived.astype(F32), axis=0).astype(BF)


def everywhere(value, axis):
    count = lax.axis_size(axis)
    copies = lax.optimization_barrier(jnp.broadcast_to(value[None], (count, *value.shape)))
    return lax.all_to_all(copies, axis, 0, 0)


def exchanged_sum(value, axis):
    return jnp.sum(everywhere(value, axis).astype(F32), axis=0).astype(BF)


def steps(edge_feats, cotangent, w_down, w_up, w_bil, basis, trip_k, trip_count, send_rows):
    edges, span = edge_feats.shape
    width = w_down.shape[1]
    trips, basis_total, _ = basis.shape
    _, blocks, slots = send_rows.shape
    reach = blocks // 2
    offsets = [j + 1 if j < reach else reach - j - 1 for j in range(blocks)]
    feats = lax.axis_size("feat")
    groups = edges // GROUP
    own_basis = basis_total // feats
    low = lambda *shape: jax.ShapeDtypeStruct(shape, BF)
    feat = lax.axis_index("feat").astype(jnp.int32)
    which = feat.reshape(1)
    sends = offsets[:feats], (offsets[feats:] + [None] * feats)[:feats]
    backs = [[None if o is None else -o for o in steps] for steps in sends]

    part_pre = dot(edge_feats, w_down).astype(BF)
    part_bar = dot(cotangent, w_up, NT).astype(BF)
    both = everywhere(jnp.concatenate([part_pre, part_bar], axis=0), "feat")

    by_basis, by_trip = call(
        prep_kernel,
        [
            jax.ShapeDtypeStruct((groups, basis_total, trips * GROUP), F32),
            jax.ShapeDtypeStruct((groups, trips, basis_total * GROUP), F32),
        ],
        [pltpu.VMEM((trips * basis_total, LANES), F32)],
        1 << 28,
        (),
        basis.reshape(trips * basis_total, edges),
        trip_count.reshape(1, edges),
    )
    k_rows = trip_k.T.reshape(trips, groups, GROUP).transpose(1, 0, 2).reshape(groups, 1, -1)

    second = jnp.minimum(feats + feat, blocks - 1)
    listed = jnp.concatenate([send_rows[0, feat], send_rows[0, second]]).reshape(-1, 1)
    pre, bar, down, out_a, out_b = call(
        down_kernel,
        [jax.ShapeDtypeStruct((edges, width), F32)]
        + [low(edges, width)] * 2
        + [low(slots, width)] * 2,
        [],
        4 * slots * edges * width,
        (),
        both,
        listed,
    )
    in_a, in_b = moved(out_a, sends[0]), moved(out_b, sends[1])

    table = edges + blocks * slots
    big = 2 * edges * trips * width * 2000
    own, rem_a, rem_b = call(
        back_kernel,
        [low(slots, width)] * 3,
        [
            pltpu.VMEM((basis_total, edges, width), BF),
            pltpu.VMEM((3 * slots, width), F32),
            pltpu.SemaphoreType.DMA((4,)),
        ],
        big,
        which,
        bar,
        k_rows,
        late=(by_trip, w_bil),
    )
    back_a = moved(rem_a, backs[0])
    back_b = moved(rem_b, backs[1])

    incoming, own = lax.optimization_barrier((jnp.concatenate([in_a, in_b], axis=0), own))
    incoming = everywhere(incoming, "feat")
    shared = everywhere(jnp.concatenate([own, back_a, back_b], axis=0), "feat")
    early = call(
        fore_kernel,
        low(own_basis * width + span, width),
        [
            pltpu.VMEM((table, width), BF),
            pltpu.VMEM((groups, trips * GROUP, width), BF),
            pltpu.VMEM((basis_total, edges, width), BF),
        ],
        big,
        which,
        down,
        incoming,
        trip_k,
        bar,
        late=(by_basis, w_bil, cotangent),
    )
    input_grad, late = call(
        last_kernel,
        [low(edges, span), low(span, width)],
        [],
        2 * edges * width * (blocks * slots + 3 * span),
        (),
        shared,
        pre,
        send_rows.reshape(1, -1),
        w_down,
        cotangent,
        edge_feats,
    )

    near = ("zl", "y", "core")
    count = lax.axis_size(near)
    pieces = [early.reshape(count, -1, width), late.reshape(count, -1, width)]
    total = scattered_sum(jnp.concatenate(pieces, axis=1), near)
    total = exchanged_sum(total, "zh")
    total = everywhere(total, near)
    factor = 1.0 / math.sqrt(edges * lax.axis_size(DOM))
    down_grad, up_grad, bil_grad = call(
        functools.partial(out_kernel, factor),
        [
            jax.ShapeDtypeStruct((span, width), F32),
            jax.ShapeDtypeStruct((width, span), F32),
            jax.ShapeDtypeStruct((own_basis * width, width), F32),
        ],
        [],
        1 << 20,
        (),
        total,
    )
    return input_grad, down_grad, up_grad, bil_grad


def solution(mesh):
    fine = Mesh(mesh.devices.reshape(4, 4, 4, 2, 4), (*DOM, "feat"))
    return jax.shard_map(
        steps,
        mesh=fine,
        in_specs=(
            P(DOM, "feat"),
            P(DOM, "feat"),
            P("feat", None),
            P(None, "feat"),
            P(),
            P(None, None, DOM),
            P(DOM, None),
            P(DOM),
            P(DOM, None, None),
        ),
        out_specs=(P(DOM, "feat"), P("feat", None), P(None, "feat"), P("feat", None)),
        check_vma=False,
    )
```

```python
import functools
import math

import jax
import jax.numpy as jnp
from jax import lax
from jax.experimental import pallas as pl
from jax.experimental.pallas import tpu as pltpu
from jax.sharding import Mesh
from jax.sharding import PartitionSpec as P

BF = jnp.bfloat16
F32 = jnp.float32
NT = (((1,), (1,)), ((), ()))
TN = (((0,), (0,)), ((), ()))
DOM = ("zh", "zl", "y", "core")
LANES = 128
BACK_UNROLL = 8
GATHER_UNROLL = 4
SUM_UNROLL = 8
VMEM_BYTES = 20 << 20
GROUP = 16


def dot(a, b, dims=(((1,), (0,)), ((), ()))):
    return lax.dot_general(a, b, dims, preferred_element_type=F32)


def ones_where(cond):
    return jnp.where(cond, 1.0, 0.0).astype(BF)


def ones_at(row, targets):
    rows = jnp.broadcast_to(row, targets.shape).astype(jnp.int16)
    return jnp.where(rows == targets.astype(jnp.int16), jnp.ones((), BF), jnp.zeros((), BF))


def iota(shape, dim):
    return lax.broadcasted_iota(jnp.int32, shape, dim)


def silu_grad(value):
    sigma = jax.nn.sigmoid(value)
    return sigma * (1.0 + value * (1.0 - sigma))


def call(kernel, outs, scratch, flops, which, *args, late=(), **more):
    moved_bytes = sum(a.size * a.dtype.itemsize for a in args)
    scalars = [pl.BlockSpec(memory_space=pltpu.SMEM)] if len(which) else []
    return pl.pallas_call(
        kernel,
        in_specs=scalars
        + [pl.BlockSpec(memory_space=pltpu.VMEM)] * len(args)
        + [pl.BlockSpec(memory_space=pltpu.HBM)] * len(late),
        out_shape=outs,
        **more,
        scratch_shapes=scratch
        + [pltpu.VMEM(a.shape, a.dtype) for a in late]
        + [pltpu.SemaphoreType.DMA] * len(late),
        compiler_params=pltpu.CompilerParams(vmem_limit_bytes=VMEM_BYTES),
        cost_estimate=pl.CostEstimate(flops=flops, bytes_accessed=moved_bytes, transcendentals=0),
    )(*([which] if len(which) else []), *args, *(pltpu.with_memory_space_constraint(a, pltpu.HBM) for a in late))


def first_kernel(feats_ref, wdown_ref, cot_ref, wup_ref, out_far, both_ref, sems):
    edges = feats_ref.shape[0]
    both_ref[:edges, :] = dot(feats_ref[...], wdown_ref[...]).astype(BF)
    both_ref[edges:, :] = dot(cot_ref[...], wup_ref[...], NT).astype(BF)
    copies = [
        pltpu.make_async_copy(both_ref, out_far.at[f], sems.at[f]) for f in range(out_far.shape[0])
    ]
    for copy in copies:
        copy.start()
    for copy in copies:
        copy.wait()


def down_kernel(both_ref, send_ref, pre_ref, bar_ref, down_ref, *out_refs):
    edges = pre_ref.shape[0]
    pre, bar = both_ref[0, :edges, :].astype(F32), both_ref[0, edges:, :].astype(F32)
    for f in range(1, both_ref.shape[0]):
        pre = pre + both_ref[f, :edges, :].astype(F32)
        bar = bar + both_ref[f, edges:, :].astype(F32)
    pre_ref[...] = pre
    bar_ref[...] = bar.astype(BF)
    down = (pre * jax.nn.sigmoid(pre)).astype(BF)
    down_ref[...] = down
    slots = out_refs[0].shape[0]
    for j, out_ref in enumerate(out_refs):
        pick = ones_where(send_ref[j * slots : (j + 1) * slots, :] == iota((slots, edges), 1))
        out_ref[...] = dot(pick, down).astype(BF)


def chunks_swapped(tiles):
    tiles = list(tiles)
    chunk = iota(tiles[0].shape, 1) // GROUP
    for step in (4, 2, 1):
        low = (chunk & step) == 0
        for i in range(8):
            if i & step:
                continue
            a, b = tiles[i], tiles[i + step]
            tiles[i] = jnp.where(low, a, pltpu.roll(b, GROUP * step, 1))
            tiles[i + step] = jnp.where(low, pltpu.roll(a, LANES - GROUP * step, 1), b)
    return tiles


def prep_kernel(basis_ref, count_ref, by_basis_ref):
    _, basis, lanes = by_basis_ref.shape
    trips = lanes // GROUP
    for t in range(count_ref.shape[1] // LANES):
        lanes = slice(t * LANES, (t + 1) * LANES)
        count = count_ref[:, lanes]
        tall = jnp.broadcast_to(count, (basis, LANES))
        for h in range(trips // 8):
            tiles = []
            for i in range(8 * h, 8 * h + 8):
                at = slice(i * basis, (i + 1) * basis)
                tiles.append(jnp.where(tall > i, basis_ref[at, lanes], 0.0))
            for q, tile in enumerate(chunks_swapped(tiles)):
                by_basis_ref[8 * t + q, :, h * LANES : (h + 1) * LANES] = tile


def diagonal(rows):
    count, lanes = rows.shape
    same = iota((GROUP, lanes), 0) == iota((GROUP, lanes), 1) % GROUP
    parts = []
    for r in range(count):
        wide = jnp.broadcast_to(rows[r : r + 1, :], (GROUP, lanes))
        parts.append(jnp.where(same, wide, 0.0).astype(BF))
    return jnp.concatenate(parts, axis=0)


def back_kernel(
    which_ref,
    bar_ref,
    k_ref,
    w_far,
    wbil_far,
    own_ref,
    rem_a_ref,
    rem_b_ref,
    grad_ref,
    acc_ref,
    part_sems,
    w_ref,
    wbil_ref,
    w_sem,
    _,
):
    basis, edges, width = grad_ref.shape
    rows = k_ref.shape[2]
    slots = own_ref.shape[0]
    fetch = pltpu.make_async_copy(w_far, w_ref, w_sem)
    soon = 4
    fetch_parts = []
    for p, at in enumerate((pl.ds(0, soon * width), pl.ds(soon * width, (basis - soon) * width))):
        fetch_parts.append(pltpu.make_async_copy(wbil_far.at[at], wbil_ref.at[at], part_sems.at[p]))
        fetch_parts[p].start()
    fetch.start()
    bar = bar_ref[...]
    for b in range(basis):
        if b in (0, soon):
            fetch_parts[b // soon].wait()
        grad_ref[b] = dot(bar, wbil_ref[b * width : (b + 1) * width, :], NT).astype(BF)
    acc_ref[...] = jnp.zeros_like(acc_ref)
    first = which_ref[0] * slots
    row = iota((3 * slots, rows), 0)
    block = row // slots
    jump = jnp.where(block == 0, 0, edges + (block - 1) * 4 * slots - block * slots)
    target = row + jump
    fetch.wait()

    def body(g, carry):
        at = pl.ds(pl.multiple_of(g * GROUP, GROUP), GROUP)
        grad = grad_ref[:, at, :].reshape(basis * GROUP, width)
        d_rows = dot(grad, diagonal(w_ref[g]), TN).astype(BF)
        acc_ref[...] += dot(d_rows, ones_at(k_ref[g] - first, target), NT)
        return carry

    lax.fori_loop(0, edges // GROUP, body, 0, unroll=BACK_UNROLL)
    for j, ref in enumerate((own_ref, rem_a_ref, rem_b_ref)):
        ref[...] = acc_ref[:, j * slots : (j + 1) * slots].T.astype(BF)


def fore_kernel(
    which_ref,
    down_ref,
    in_ref,
    k_ref,
    bar_ref,
    w_far,
    wbil_far,
    cot_far,
    term_ref,
    tab_ref,
    got_ref,
    sum_ref,
    w_ref,
    wbil_ref,
    cot_ref,
    w_sem,
    wbil_sem,
    cot_sem,
):
    fetch_w = pltpu.make_async_copy(w_far, w_ref, w_sem)
    fetch_wbil = pltpu.make_async_copy(wbil_far, wbil_ref, wbil_sem)
    fetch_cot = pltpu.make_async_copy(cot_far, cot_ref, cot_sem)
    fetch_w.start()
    fetch_wbil.start()
    fetch_cot.start()
    groups, width, rows = got_ref.shape
    basis, edges, _ = sum_ref.shape
    table = tab_ref.shape[1]
    slots = in_ref.shape[1] // 2
    parts = [down_ref[j * slots : (j + 1) * slots, :] for j in range(edges // slots)]
    parts += [in_ref[f, :slots, :] for f in range(4)] + [in_ref[f, slots:, :] for f in range(2)]
    for j, part in enumerate(parts):
        tab_ref[:, j * slots : (j + 1) * slots] = part.astype(F32).T.astype(BF)

    def gather(g, carry):
        pick = ones_at(k_ref[g], iota((table, rows), 0))
        got_ref[g] = dot(tab_ref[...], pick).astype(BF)
        return carry

    lax.fori_loop(0, groups, gather, 0, unroll=GATHER_UNROLL)
    fetch_w.wait()

    def add_up(g, carry):
        at = pl.ds(pl.multiple_of(g * GROUP, GROUP), GROUP)
        total = dot(diagonal(w_ref[g]), got_ref[g], NT).astype(BF)
        sum_ref[:, at, :] = total.reshape(basis, GROUP, width)
        return carry

    lax.fori_loop(0, groups, add_up, 0, unroll=SUM_UNROLL)
    fetch_wbil.wait()
    fetch_cot.wait()
    agg = jnp.zeros((width, edges), F32)
    for b in range(0, basis, 2):
        pair = jnp.concatenate([sum_ref[b], sum_ref[b + 1]], axis=1)
        agg = agg + dot(wbil_ref[:, b * width : (b + 2) * width], pair, NT)
    agg = agg.astype(BF)
    bar = bar_ref[...]
    own = term_ref.shape[0] // width - cot_ref.shape[1] // width
    for j in range(own):
        part = dot(sum_ref[which_ref[0] * own + j], bar, TN)
        term_ref[j * width : (j + 1) * width, :] = part.astype(BF)
    for h in range(cot_ref.shape[1] // width):
        up = dot(agg, cot_ref[:, h * width : (h + 1) * width])
        term_ref[(own + h) * width : (own + h + 1) * width, :] = up.astype(BF)


def last_kernel(got_ref, pre_ref, send_ref, wdown_ref, cot_ref, feats_ref, grad_ref, term_ref):
    edges, span = cot_ref.shape
    share = edges // got_ref.shape[0]
    feats = got_ref.shape[0]
    part = lambda j: [got_ref[f, j * share : (j + 1) * share, :] for f in range(feats)]
    blocks = part(1) + part(2)
    count = send_ref.shape[1] // share
    total = jnp.concatenate(part(0), axis=0).astype(F32)
    place = ones_where(send_ref[...] == iota((edges, count * share), 0))
    total = total + dot(place, jnp.concatenate(blocks[:count], axis=0))
    pre_bar = (total * silu_grad(pre_ref[...])).astype(BF)
    grad_ref[...] = (cot_ref[...].astype(F32) + dot(pre_bar, wdown_ref[...], NT)).astype(BF)
    term_ref[...] = dot(feats_ref[...], pre_bar, TN).astype(BF)


def out_kernel(factor, total_ref, down_ref, up_ref, bil_ref):
    pieces, rows, width = total_ref.shape
    late = down_ref.shape[0] // pieces
    early = rows - late
    full = total_ref[...].astype(F32) * factor
    down_ref[...] = full[:, early:, :].reshape(down_ref.shape)
    flat = full[:, :early, :].reshape(pieces * early, width)
    own = bil_ref.shape[0]
    bil_ref[...] = flat[:own, :]
    for h in range(up_ref.shape[1] // width):
        up_ref[:, h * width : (h + 1) * width] = flat[own + h * width : own + (h + 1) * width, :]


def moved(value, steps):
    domains, feats = lax.axis_size(DOM), lax.axis_size("feat")
    pairs = [
        (d * feats + f, (d + step) % domains * feats + f)
        for d in range(domains)
        for f, step in enumerate(steps[:feats])
        if step is not None
    ]
    return lax.ppermute(value, (*DOM, "feat"), pairs)


def scattered_sum(pieces, axis):
    arrived = lax.all_to_all(pieces, axis, 0, 0)
    return jnp.sum(arrived.astype(F32), axis=0).astype(BF)


def everywhere(value, axis):
    count = lax.axis_size(axis)
    copies = lax.optimization_barrier(jnp.broadcast_to(value[None], (count, *value.shape)))
    return lax.all_to_all(copies, axis, 0, 0)


def exchanged_sum(value, axis):
    return jnp.sum(everywhere(value, axis).astype(F32), axis=0).astype(BF)


def local(edge_feats, cotangent, w_down, w_up, w_bil, basis, trip_k, trip_count, send_rows):
    edges, span = edge_feats.shape
    width = w_down.shape[1]
    trips, basis_total, _ = basis.shape
    _, blocks, slots = send_rows.shape
    reach = blocks // 2
    offsets = [j + 1 if j < reach else reach - j - 1 for j in range(blocks)]
    feats = lax.axis_size("feat")
    groups = edges // GROUP
    own_basis = basis_total // feats
    low = lambda *shape: jax.ShapeDtypeStruct(shape, BF)
    feat = lax.axis_index("feat").astype(jnp.int32)
    which = feat.reshape(1)
    sends = offsets[:feats], (offsets[feats:] + [None] * feats)[:feats]
    backs = [[None if o is None else -o for o in steps] for steps in sends]

    both = call(
        first_kernel,
        low(feats, 2 * edges, width),
        [pltpu.VMEM((2 * edges, width), BF), pltpu.SemaphoreType.DMA((feats,))],
        4 * edges * span * width,
        (),
        edge_feats,
        w_down,
        cotangent,
        w_up,
        out_specs=pl.BlockSpec(memory_space=pltpu.HBM),
    )
    both = lax.all_to_all(both, "feat", 0, 0)

    by_basis = call(
        prep_kernel,
        jax.ShapeDtypeStruct((groups, basis_total, trips * GROUP), F32),
        [],
        1 << 28,
        (),
        basis.reshape(trips * basis_total, edges),
        trip_count.reshape(1, edges),
    )
    k_rows = trip_k.T.reshape(trips, groups, GROUP).transpose(1, 0, 2).reshape(groups, 1, -1)

    second = jnp.minimum(feats + feat, blocks - 1)
    listed = jnp.concatenate([send_rows[0, feat], send_rows[0, second]]).reshape(-1, 1)
    pre, bar, down, out_a, out_b = call(
        down_kernel,
        [jax.ShapeDtypeStruct((edges, width), F32)]
        + [low(edges, width)] * 2
        + [low(slots, width)] * 2,
        [],
        4 * slots * edges * width,
        (),
        both,
        listed,
    )
    in_a, in_b = moved(out_a, sends[0]), moved(out_b, sends[1])

    table = edges + blocks * slots
    big = 2 * edges * trips * width * 2000
    own, rem_a, rem_b = call(
        back_kernel,
        [low(slots, width)] * 3,
        [
            pltpu.VMEM((basis_total, edges, width), BF),
            pltpu.VMEM((width, 3 * slots), F32),
            pltpu.SemaphoreType.DMA((2,)),
        ],
        big,
        which,
        bar,
        k_rows,
        late=(by_basis, w_bil),
    )
    back_a, back_b = moved(rem_a, backs[0]), moved(rem_b, backs[1])

    incoming, own = lax.optimization_barrier((jnp.concatenate([in_a, in_b], axis=0), own))
    incoming = everywhere(incoming, "feat")
    shared = everywhere(jnp.concatenate([own, back_a, back_b], axis=0), "feat")
    early = call(
        fore_kernel,
        low(own_basis * width + span, width),
        [
            pltpu.VMEM((width, table), BF),
            pltpu.VMEM((groups, width, trips * GROUP), BF),
            pltpu.VMEM((basis_total, edges, width), BF),
        ],
        big,
        which,
        down,
        incoming,
        k_rows,
        bar,
        late=(by_basis, w_bil.T, cotangent),
    )
    input_grad, late = call(
        last_kernel,
        [low(edges, span), low(span, width)],
        [],
        2 * edges * width * (blocks * slots + 3 * span),
        (),
        shared,
        pre,
        send_rows.reshape(1, -1),
        w_down,
        cotangent,
        edge_feats,
    )

    near = ("zl", "y", "core")
    count = lax.axis_size(near)
    pieces = [early.reshape(count, -1, width), late.reshape(count, -1, width)]
    total = scattered_sum(jnp.concatenate(pieces, axis=1), near)
    total = exchanged_sum(total, "zh")
    total = everywhere(total, near)
    factor = 1.0 / math.sqrt(edges * lax.axis_size(DOM))
    down_grad, up_grad, bil_grad = call(
        functools.partial(out_kernel, factor),
        [
            jax.ShapeDtypeStruct((span, width), F32),
            jax.ShapeDtypeStruct((width, span), F32),
            jax.ShapeDtypeStruct((own_basis * width, width), F32),
        ],
        [],
        1 << 20,
        (),
        total,
    )
    return input_grad, down_grad, up_grad, bil_grad


def solution(mesh):
    fine = Mesh(mesh.devices.reshape(4, 4, 4, 2, 4), (*DOM, "feat"))
    return jax.shard_map(
        local,
        mesh=fine,
        in_specs=(
            P(DOM, "feat"),
            P(DOM, "feat"),
            P("feat", None),
            P(None, "feat"),
            P(),
            P(None, None, DOM),
            P(DOM, None),
            P(DOM),
            P(DOM, None, None),
        ),
        out_specs=(P(DOM, "feat"), P("feat", None), P(None, "feat"), P("feat", None)),
        check_vma=False,
    )
```

```python
import functools
import math

import jax
import jax.numpy as jnp
from jax import lax
from jax.experimental import pallas as pl
from jax.experimental.pallas import tpu as pltpu
from jax.sharding import Mesh
from jax.sharding import PartitionSpec as P

BF = jnp.bfloat16
F32 = jnp.float32
NT = (((1,), (1,)), ((), ()))
TN = (((0,), (0,)), ((), ()))
DOM = ("zh", "zl", "y", "core")
LANES = 128
BACK_UNROLL = 8
GATHER_UNROLL = 4
SUM_UNROLL = 8
VMEM_BYTES = 20 << 20
GROUP = 16


PLAIN = (((1,), (0,)), ((), ()))


def dot(a, b, dims=PLAIN):
    return lax.dot_general(a, b, dims, preferred_element_type=F32)


def ones_where(cond):
    return jnp.where(cond, 1.0, 0.0).astype(BF)


def ones_at(row, targets):
    rows = jnp.broadcast_to(row, targets.shape).astype(jnp.int16)
    return jnp.where(rows == targets.astype(jnp.int16), jnp.ones((), BF), jnp.zeros((), BF))


def iota(shape, dim):
    return lax.broadcasted_iota(jnp.int32, shape, dim)


def silu_grad(value):
    sigma = jax.nn.sigmoid(value)
    return sigma * (1.0 + value * (1.0 - sigma))


def call(kernel, outs, scratch, flops, which, *args, late=(), **more):
    moved_bytes = sum(a.size * a.dtype.itemsize for a in args)
    scalars = [pl.BlockSpec(memory_space=pltpu.SMEM)] if len(which) else []
    return pl.pallas_call(
        kernel,
        in_specs=scalars
        + [pl.BlockSpec(memory_space=pltpu.VMEM)] * len(args)
        + [pl.BlockSpec(memory_space=pltpu.HBM)] * len(late),
        out_shape=outs,
        **more,
        scratch_shapes=scratch
        + [pltpu.VMEM(a.shape, a.dtype) for a in late]
        + [pltpu.SemaphoreType.DMA] * len(late),
        compiler_params=pltpu.CompilerParams(vmem_limit_bytes=VMEM_BYTES),
        cost_estimate=pl.CostEstimate(flops=flops, bytes_accessed=moved_bytes, transcendentals=0),
    )(*([which] if len(which) else []), *args, *(pltpu.with_memory_space_constraint(a, pltpu.HBM) for a in late))


def first_kernel(feats_far, wdown_far, cot_far, wup_far, out_far, both_ref, sems, *fetched):
    refs, in_sems = fetched[:4], fetched[4:]
    fars = feats_far, wdown_far, cot_far, wup_far
    fetches = [pltpu.make_async_copy(*trio) for trio in zip(fars, refs, in_sems)]
    for fetch in fetches:
        fetch.start()
    count, rows, _ = out_far.shape
    half = rows // 2
    copies = []
    for h, dims in enumerate((PLAIN, NT)):
        fetches[2 * h].wait()
        fetches[2 * h + 1].wait()
        part = pl.ds(h * half, half)
        both_ref[part, :] = dot(refs[2 * h][...], refs[2 * h + 1][...], dims).astype(BF)
        for f in range(count):
            far = out_far.at[f, part]
            copies.append(pltpu.make_async_copy(both_ref.at[part], far, sems.at[h, f]))
            copies[-1].start()
    for copy in copies:
        copy.wait()


def summed_over(parts_ref, rows):
    total = parts_ref[0, rows, :].astype(F32)
    for f in range(1, parts_ref.shape[0]):
        total = total + parts_ref[f, rows, :].astype(F32)
    return total


def down_kernel(parts_ref, send_ref, pre_ref, bar_ref, down_ref, *out_refs):
    edges = pre_ref.shape[0]
    pre = summed_over(parts_ref, pl.ds(0, edges))
    pre_ref[...] = pre
    bar_ref[...] = summed_over(parts_ref, pl.ds(edges, edges)).astype(BF)
    down = (pre * jax.nn.sigmoid(pre)).astype(BF)
    down_ref[...] = down
    slots = out_refs[0].shape[0]
    for j, out_ref in enumerate(out_refs):
        pick = ones_where(send_ref[j * slots : (j + 1) * slots, :] == iota((slots, edges), 1))
        out_ref[...] = dot(pick, down).astype(BF)


def chunks_swapped(tiles):
    tiles = list(tiles)
    chunk = iota(tiles[0].shape, 1) // GROUP
    for step in (4, 2, 1):
        low = (chunk & step) == 0
        for i in range(8):
            if i & step:
                continue
            a, b = tiles[i], tiles[i + step]
            tiles[i] = jnp.where(low, a, pltpu.roll(b, GROUP * step, 1))
            tiles[i + step] = jnp.where(low, pltpu.roll(a, LANES - GROUP * step, 1), b)
    return tiles


def prep_kernel(basis_ref, count_ref, wbil_ref, by_basis_ref, by_trip_ref, turned_ref, live_ref):
    _, basis, _ = by_basis_ref.shape
    _, trips, _ = by_trip_ref.shape
    for t in range(count_ref.shape[1] // LANES):
        lanes = slice(t * LANES, (t + 1) * LANES)
        count = count_ref[:, lanes]
        tall = jnp.broadcast_to(count, (basis, LANES))
        for h in range(trips // 8):
            tiles = []
            for i in range(8 * h, 8 * h + 8):
                at = slice(i * basis, (i + 1) * basis)
                tiles.append(jnp.where(tall > i, basis_ref[at, lanes], 0.0))
                live_ref[at, :] = tiles[-1]
            for q, tile in enumerate(chunks_swapped(tiles)):
                by_basis_ref[8 * t + q, :, h * LANES : (h + 1) * LANES] = tile
        for o in range(basis // 8):
            octet = range(8 * o, 8 * o + 8)
            tiles = [live_ref[pl.ds(b, trips, stride=basis), :] for b in octet]
            for q, tile in enumerate(chunks_swapped(tiles)):
                by_trip_ref[8 * t + q, :, o * LANES : (o + 1) * LANES] = tile
    for b in range(basis):
        block = slice(b * LANES, (b + 1) * LANES)
        turned_ref[:, block] = wbil_ref[block, :].astype(F32).T.astype(BF)


def diagonal(rows):
    count, lanes = rows.shape
    same = iota((GROUP, lanes), 0) == iota((GROUP, lanes), 1) % GROUP
    parts = []
    for r in range(count):
        wide = jnp.broadcast_to(rows[r : r + 1, :], (GROUP, lanes))
        parts.append(jnp.where(same, wide, 0.0).astype(BF))
    return jnp.concatenate(parts, axis=0)


def back_kernel(
    which_ref,
    bar_ref,
    k_ref,
    w_ref,
    wbil_far,
    own_ref,
    rem_a_ref,
    rem_b_ref,
    grad_ref,
    acc_ref,
    part_sems,
    wbil_ref,
    _,
):
    basis, edges, width = grad_ref.shape
    rows = k_ref.shape[2]
    slots = own_ref.shape[0]
    soon = 4
    fetch_parts = []
    for p, at in enumerate((pl.ds(0, soon * width), pl.ds(soon * width, (basis - soon) * width))):
        fetch_parts.append(pltpu.make_async_copy(wbil_far.at[at], wbil_ref.at[at], part_sems.at[p]))
        fetch_parts[p].start()
    bar = bar_ref[...]
    for b in range(basis):
        if b in (0, soon):
            fetch_parts[b // soon].wait()
        grad_ref[b] = dot(bar, wbil_ref[b * width : (b + 1) * width, :], NT).astype(BF)
    acc_ref[...] = jnp.zeros_like(acc_ref)
    first = which_ref[0] * slots
    row = iota((3 * slots, rows), 0)
    block = row // slots
    jump = jnp.where(block == 0, 0, edges + (block - 1) * 4 * slots - block * slots)
    target = row + jump

    def body(g, carry):
        at = pl.ds(pl.multiple_of(g * GROUP, GROUP), GROUP)
        grad = grad_ref[:, at, :].reshape(basis * GROUP, width)
        d_rows = dot(diagonal(w_ref[g]), grad).astype(BF)
        acc_ref[...] += dot(ones_at(k_ref[g] - first, target), d_rows)
        return carry

    lax.fori_loop(0, edges // GROUP, body, 0, unroll=BACK_UNROLL)
    for j, ref in enumerate((own_ref, rem_a_ref, rem_b_ref)):
        ref[...] = acc_ref[j * slots : (j + 1) * slots, :].astype(BF)


def fore_kernel(
    which_ref,
    down_ref,
    in_ref,
    k_ref,
    bar_ref,
    w_far,
    wbil_far,
    cot_far,
    term_ref,
    tab_ref,
    got_ref,
    sum_ref,
    w_ref,
    wbil_ref,
    cot_ref,
    w_sem,
    wbil_sem,
    cot_sem,
):
    fetch_w = pltpu.make_async_copy(w_far, w_ref, w_sem)
    fetch_wbil = pltpu.make_async_copy(wbil_far, wbil_ref, wbil_sem)
    fetch_cot = pltpu.make_async_copy(cot_far, cot_ref, cot_sem)
    fetch_w.start()
    fetch_wbil.start()
    fetch_cot.start()
    groups, width, rows = got_ref.shape
    basis, edges, _ = sum_ref.shape
    table = tab_ref.shape[1]
    slots = in_ref.shape[1] // 2
    parts = [down_ref[j * slots : (j + 1) * slots, :] for j in range(edges // slots)]
    parts += [in_ref[f, :slots, :] for f in range(4)] + [in_ref[f, slots:, :] for f in range(2)]
    for j, part in enumerate(parts):
        tab_ref[:, j * slots : (j + 1) * slots] = part.astype(F32).T.astype(BF)

    def gather(g, carry):
        pick = ones_at(k_ref[g], iota((table, rows), 0))
        got_ref[g] = dot(tab_ref[...], pick).astype(BF)
        return carry

    lax.fori_loop(0, groups, gather, 0, unroll=GATHER_UNROLL)
    fetch_w.wait()

    def add_up(g, carry):
        at = pl.ds(pl.multiple_of(g * GROUP, GROUP), GROUP)
        total = dot(diagonal(w_ref[g]), got_ref[g], NT).astype(BF)
        sum_ref[:, at, :] = total.reshape(basis, GROUP, width)
        return carry

    lax.fori_loop(0, groups, add_up, 0, unroll=SUM_UNROLL)
    fetch_wbil.wait()
    fetch_cot.wait()
    agg = jnp.zeros((width, edges), F32)
    for b in range(0, basis, 2):
        pair = jnp.concatenate([sum_ref[b], sum_ref[b + 1]], axis=1)
        agg = agg + dot(wbil_ref[:, b * width : (b + 2) * width], pair, NT)
    agg = agg.astype(BF)
    bar = bar_ref[...]
    own = term_ref.shape[0] // width - cot_ref.shape[1] // width
    for j in range(own):
        part = dot(sum_ref[which_ref[0] * own + j], bar, TN)
        term_ref[j * width : (j + 1) * width, :] = part.astype(BF)
    for h in range(cot_ref.shape[1] // width):
        up = dot(agg, cot_ref[:, h * width : (h + 1) * width])
        term_ref[(own + h) * width : (own + h + 1) * width, :] = up.astype(BF)


def last_kernel(got_ref, pre_ref, send_ref, wdown_ref, cot_ref, feats_ref, grad_ref, term_ref):
    edges, span = cot_ref.shape
    share = edges // got_ref.shape[0]
    feats = got_ref.shape[0]
    part = lambda j: [got_ref[f, j * share : (j + 1) * share, :] for f in range(feats)]
    blocks = part(1) + part(2)
    count = send_ref.shape[1] // share
    total = jnp.concatenate(part(0), axis=0).astype(F32)
    place = ones_where(send_ref[...] == iota((edges, count * share), 0))
    total = total + dot(place, jnp.concatenate(blocks[:count], axis=0))
    pre_bar = (total * silu_grad(pre_ref[...])).astype(BF)
    grad_ref[...] = (cot_ref[...].astype(F32) + dot(pre_bar, wdown_ref[...], NT)).astype(BF)
    term_ref[...] = dot(feats_ref[...], pre_bar, TN).astype(BF)


def out_kernel(factor, total_ref, down_ref, up_ref, bil_ref):
    pieces, rows, width = total_ref.shape
    late = down_ref.shape[0] // pieces
    early = rows - late
    full = total_ref[...].astype(F32) * factor
    down_ref[...] = full[:, early:, :].reshape(down_ref.shape)
    flat = full[:, :early, :].reshape(pieces * early, width)
    own = bil_ref.shape[0]
    bil_ref[...] = flat[:own, :]
    for h in range(up_ref.shape[1] // width):
        up_ref[:, h * width : (h + 1) * width] = flat[own + h * width : own + (h + 1) * width, :]


def moved(value, steps):
    domains, feats = lax.axis_size(DOM), lax.axis_size("feat")
    pairs = [
        (d * feats + f, (d + step) % domains * feats + f)
        for d in range(domains)
        for f, step in enumerate(steps[:feats])
        if step is not None
    ]
    return lax.ppermute(value, (*DOM, "feat"), pairs)


def scattered_sum(pieces, axis):
    arrived = lax.all_to_all(pieces, axis, 0, 0)
    return jnp.sum(arrived.astype(F32), axis=0).astype(BF)


def everywhere(value, axis):
    count = lax.axis_size(axis)
    copies = lax.optimization_barrier(jnp.broadcast_to(value[None], (count, *value.shape)))
    return lax.all_to_all(copies, axis, 0, 0)


def exchanged_sum(value, axis):
    return jnp.sum(everywhere(value, axis).astype(F32), axis=0).astype(BF)


def local(edge_feats, cotangent, w_down, w_up, w_bil, basis, trip_k, trip_count, send_rows):
    edges, span = edge_feats.shape
    width = w_down.shape[1]
    trips, basis_total, _ = basis.shape
    _, blocks, slots = send_rows.shape
    reach = blocks // 2
    offsets = [j + 1 if j < reach else reach - j - 1 for j in range(blocks)]
    feats = lax.axis_size("feat")
    groups = edges // GROUP
    own_basis = basis_total // feats
    low = lambda *shape: jax.ShapeDtypeStruct(shape, BF)
    feat = lax.axis_index("feat").astype(jnp.int32)
    which = feat.reshape(1)
    sends = offsets[:feats], (offsets[feats:] + [None] * feats)[:feats]
    backs = [[None if o is None else -o for o in steps] for steps in sends]

    both = call(
        first_kernel,
        low(feats, 2 * edges, width),
        [pltpu.VMEM((2 * edges, width), BF), pltpu.SemaphoreType.DMA((2, feats))],
        4 * edges * span * width,
        (),
        late=(edge_feats, w_down, cotangent, w_up),
        out_specs=pl.BlockSpec(memory_space=pltpu.HBM),
    )
    both = lax.all_to_all(both, "feat", 0, 0)

    by_basis, by_trip, turned = call(
        prep_kernel,
        [
            jax.ShapeDtypeStruct((groups, basis_total, trips * GROUP), F32),
            jax.ShapeDtypeStruct((groups, trips, basis_total * GROUP), F32),
            low(width, basis_total * width),
        ],
        [pltpu.VMEM((trips * basis_total, LANES), F32)],
        1 << 28,
        (),
        basis.reshape(trips * basis_total, edges),
        trip_count.reshape(1, edges),
        w_bil,
    )
    k_rows = trip_k.T.reshape(trips, groups, GROUP).transpose(1, 0, 2).reshape(groups, 1, -1)

    second = jnp.minimum(feats + feat, blocks - 1)
    listed = jnp.concatenate([send_rows[0, feat], send_rows[0, second]]).reshape(-1, 1)
    pre, bar, down, out_a, out_b = call(
        down_kernel,
        [
            jax.ShapeDtypeStruct((edges, width), F32),
            low(edges, width),
            low(edges, width),
            low(slots, width),
            low(slots, width),
        ],
        [],
        4 * slots * edges * width,
        (),
        both,
        listed,
    )
    in_a, in_b = moved(out_a, sends[0]), moved(out_b, sends[1])

    table = edges + blocks * slots
    big = 2 * edges * trips * width * 2000
    own, rem_a, rem_b = call(
        back_kernel,
        [low(slots, width)] * 3,
        [
            pltpu.VMEM((basis_total, edges, width), BF),
            pltpu.VMEM((3 * slots, width), F32),
            pltpu.SemaphoreType.DMA((2,)),
        ],
        big,
        which,
        bar,
        k_rows,
        by_trip,
        late=(w_bil,),
    )
    back_a, back_b = moved(rem_a, backs[0]), moved(rem_b, backs[1])

    incoming, own = lax.optimization_barrier((jnp.concatenate([in_a, in_b], axis=0), own))
    incoming = everywhere(incoming, "feat")
    shared = everywhere(jnp.concatenate([own, back_a, back_b], axis=0), "feat")
    early = call(
        fore_kernel,
        low(own_basis * width + span, width),
        [
            pltpu.VMEM((width, table), BF),
            pltpu.VMEM((groups, width, trips * GROUP), BF),
            pltpu.VMEM((basis_total, edges, width), BF),
        ],
        big,
        which,
        down,
        incoming,
        k_rows,
        bar,
        late=(by_basis, turned, cotangent),
    )
    input_grad, late = call(
        last_kernel,
        [low(edges, span), low(span, width)],
        [],
        2 * edges * width * (blocks * slots + 3 * span),
        (),
        shared,
        pre,
        send_rows.reshape(1, -1),
        w_down,
        cotangent,
        edge_feats,
    )

    near = ("zl", "y", "core")
    count = lax.axis_size(near)
    pieces = [early.reshape(count, -1, width), late.reshape(count, -1, width)]
    total = scattered_sum(jnp.concatenate(pieces, axis=1), near)
    total = exchanged_sum(total, "zh")
    total = everywhere(total, near)
    factor = 1.0 / math.sqrt(edges * lax.axis_size(DOM))
    down_grad, up_grad, bil_grad = call(
        functools.partial(out_kernel, factor),
        [
            jax.ShapeDtypeStruct((span, width), F32),
            jax.ShapeDtypeStruct((width, span), F32),
            jax.ShapeDtypeStruct((own_basis * width, width), F32),
        ],
        [],
        1 << 20,
        (),
        total,
    )
    return input_grad, down_grad, up_grad, bil_grad


def solution(mesh):
    fine = Mesh(mesh.devices.reshape(8, 2, 4, 2, 4), (*DOM, "feat"))
    return jax.shard_map(
        local,
        mesh=fine,
        in_specs=(
            P(DOM, "feat"),
            P(DOM, "feat"),
            P("feat", None),
            P(None, "feat"),
            P(),
            P(None, None, DOM),
            P(DOM, None),
            P(DOM),
            P(DOM, None, None),
        ),
        out_specs=(P(DOM, "feat"), P("feat", None), P(None, "feat"), P("feat", None)),
        check_vma=False,
    )
```

```python
import functools
import math

import jax
import jax.numpy as jnp
from jax import lax
from jax.experimental import pallas as pl
from jax.experimental.pallas import tpu as pltpu
from jax.sharding import Mesh
from jax.sharding import PartitionSpec as P

BF = jnp.bfloat16
F32 = jnp.float32
NT = (((1,), (1,)), ((), ()))
TN = (((0,), (0,)), ((), ()))
DOM = ("zh", "zl", "y", "core")
LANES = 128
BACK_UNROLL = 8
CHUNKS = (0, 4, 8, 16)
STAGES = 8
GATHER_UNROLL = 4
VMEM_BYTES = 20 << 20
GROUP = 16


PLAIN = (((1,), (0,)), ((), ()))


def dot(a, b, dims=PLAIN):
    return lax.dot_general(a, b, dims, preferred_element_type=F32)


def ones_where(cond):
    return jnp.where(cond, 1.0, 0.0).astype(BF)


def ones_at(row, targets):
    rows = jnp.broadcast_to(row, targets.shape).astype(jnp.int16)
    return jnp.where(rows == targets.astype(jnp.int16), jnp.ones((), BF), jnp.zeros((), BF))


def iota(shape, dim):
    return lax.broadcasted_iota(jnp.int32, shape, dim)


def silu_grad(value):
    sigma = jax.nn.sigmoid(value)
    return sigma * (1.0 + value * (1.0 - sigma))


def call(kernel, outs, scratch, flops, which, *args, late=(), **more):
    moved_bytes = sum(a.size * a.dtype.itemsize for a in args)
    scalars = [pl.BlockSpec(memory_space=pltpu.SMEM)] if len(which) else []
    return pl.pallas_call(
        kernel,
        in_specs=scalars
        + [pl.BlockSpec(memory_space=pltpu.VMEM)] * len(args)
        + [pl.BlockSpec(memory_space=pltpu.HBM)] * len(late),
        out_shape=outs,
        **more,
        scratch_shapes=scratch
        + [pltpu.VMEM(a.shape, a.dtype) for a in late]
        + [pltpu.SemaphoreType.DMA] * len(late),
        compiler_params=pltpu.CompilerParams(vmem_limit_bytes=VMEM_BYTES),
        cost_estimate=pl.CostEstimate(flops=flops, bytes_accessed=moved_bytes, transcendentals=0),
    )(*([which] if len(which) else []), *args, *(pltpu.with_memory_space_constraint(a, pltpu.HBM) for a in late))


def first_kernel(feats_far, wdown_far, cot_far, wup_far, out_far, both_ref, sems, *fetched):
    refs, in_sems = fetched[:4], fetched[4:]
    fars = feats_far, wdown_far, cot_far, wup_far
    fetches = [pltpu.make_async_copy(*trio) for trio in zip(fars, refs, in_sems)]
    for fetch in fetches:
        fetch.start()
    count, rows, _ = out_far.shape
    half = rows // 2
    copies = []
    for h, dims in enumerate((PLAIN, NT)):
        fetches[2 * h].wait()
        fetches[2 * h + 1].wait()
        part = pl.ds(h * half, half)
        both_ref[part, :] = dot(refs[2 * h][...], refs[2 * h + 1][...], dims).astype(BF)
        for f in range(count):
            far = out_far.at[f, part]
            copies.append(pltpu.make_async_copy(both_ref.at[part], far, sems.at[h, f]))
            copies[-1].start()
    for copy in copies:
        copy.wait()


def summed_over(parts_ref, rows):
    total = parts_ref[0, rows, :].astype(F32)
    for f in range(1, parts_ref.shape[0]):
        total = total + parts_ref[f, rows, :].astype(F32)
    return total


def down_kernel(parts_ref, send_ref, pre_ref, bar_ref, down_ref, *out_refs):
    edges = pre_ref.shape[0]
    pre = summed_over(parts_ref, pl.ds(0, edges))
    pre_ref[...] = pre
    bar_ref[...] = summed_over(parts_ref, pl.ds(edges, edges)).astype(BF)
    down = (pre * jax.nn.sigmoid(pre)).astype(BF)
    down_ref[...] = down
    slots = out_refs[0].shape[0]
    for j, out_ref in enumerate(out_refs):
        pick = ones_where(send_ref[j * slots : (j + 1) * slots, :] == iota((slots, edges), 1))
        out_ref[...] = dot(pick, down).astype(BF)


def chunks_swapped(tiles):
    tiles = list(tiles)
    chunk = iota(tiles[0].shape, 1) // GROUP
    for step in (4, 2, 1):
        low = (chunk & step) == 0
        for i in range(8):
            if i & step:
                continue
            a, b = tiles[i], tiles[i + step]
            tiles[i] = jnp.where(low, a, pltpu.roll(b, GROUP * step, 1))
            tiles[i + step] = jnp.where(low, pltpu.roll(a, LANES - GROUP * step, 1), b)
    return tiles


def prep_kernel(basis_ref, count_ref, wbil_ref, by_basis_ref, by_trip_ref, turned_ref, live_ref):
    _, basis, _ = by_basis_ref.shape
    _, trips, _ = by_trip_ref.shape
    for t in range(count_ref.shape[1] // LANES):
        lanes = slice(t * LANES, (t + 1) * LANES)
        count = count_ref[:, lanes]
        tall = jnp.broadcast_to(count, (basis, LANES))
        for h in range(trips // 8):
            tiles = []
            for i in range(8 * h, 8 * h + 8):
                at = slice(i * basis, (i + 1) * basis)
                tiles.append(jnp.where(tall > i, basis_ref[at, lanes], 0.0))
                live_ref[at, :] = tiles[-1]
            for q, tile in enumerate(chunks_swapped(tiles)):
                by_basis_ref[8 * t + q, :, h * LANES : (h + 1) * LANES] = tile
        for o in range(basis // 8):
            octet = range(8 * o, 8 * o + 8)
            tiles = [live_ref[pl.ds(b, trips, stride=basis), :] for b in octet]
            for q, tile in enumerate(chunks_swapped(tiles)):
                by_trip_ref[8 * t + q, :, o * LANES : (o + 1) * LANES] = tile
    for b in range(basis):
        block = slice(b * LANES, (b + 1) * LANES)
        turned_ref[:, block] = wbil_ref[block, :].astype(F32).T.astype(BF)


def diagonal(rows):
    count, lanes = rows.shape
    same = iota((GROUP, lanes), 0) == iota((GROUP, lanes), 1) % GROUP
    parts = []
    for r in range(count):
        wide = jnp.broadcast_to(rows[r : r + 1, :], (GROUP, lanes))
        parts.append(jnp.where(same, wide, 0.0).astype(BF))
    return jnp.concatenate(parts, axis=0)


def back_kernel(
    which_ref,
    bar_ref,
    k_ref,
    w_far,
    wbil_far,
    own_ref,
    rem_a_ref,
    rem_b_ref,
    grad_ref,
    acc_ref,
    part_sems,
    w_ref,
    wbil_ref,
    w_sem,
    _,
):
    basis, edges, width = grad_ref.shape
    rows = k_ref.shape[2]
    slots = own_ref.shape[0]
    fetches = {}
    for p, (b, stop) in enumerate(zip(CHUNKS, (*CHUNKS[1:], basis))):
        at = pl.ds(b * width, (stop - b) * width)
        fetches[b] = pltpu.make_async_copy(wbil_far.at[at], wbil_ref.at[at], part_sems.at[p])
        fetches[b].start()
    fetch_w = pltpu.make_async_copy(w_far, w_ref, w_sem)
    fetch_w.start()
    bar = bar_ref[...]
    for b in range(basis):
        if b in fetches:
            fetches[b].wait()
        grad_ref[b] = dot(bar, wbil_ref[b * width : (b + 1) * width, :], NT).astype(BF)
    acc_ref[...] = jnp.zeros_like(acc_ref)
    first = which_ref[0] * slots
    row = iota((3 * slots, rows), 0)
    block = row // slots
    jump = jnp.where(block == 0, 0, edges + (block - 1) * 4 * slots - block * slots)
    target = row + jump
    fetch_w.wait()

    def body(g, carry):
        at = pl.ds(pl.multiple_of(g * GROUP, GROUP), GROUP)
        grad = grad_ref[:, at, :].reshape(basis * GROUP, width)
        d_rows = dot(diagonal(w_ref[g]), grad).astype(BF)
        acc_ref[...] += dot(ones_at(k_ref[g] - first, target), d_rows)
        return carry

    lax.fori_loop(0, edges // GROUP, body, 0, unroll=BACK_UNROLL)
    for j, ref in enumerate((own_ref, rem_a_ref, rem_b_ref)):
        ref[...] = acc_ref[j * slots : (j + 1) * slots, :].astype(BF)


def gather_kernel(down_ref, in_ref, k_ref, got_far, tab_ref, got_ref, sems):
    groups, _, rows = got_ref.shape
    edges = down_ref.shape[0]
    table = tab_ref.shape[1]
    slots = in_ref.shape[1] // 2
    parts = [down_ref[j * slots : (j + 1) * slots, :] for j in range(edges // slots)]
    parts += [in_ref[f, :slots, :] for f in range(4)] + [in_ref[f, slots:, :] for f in range(2)]
    for j, part in enumerate(parts):
        tab_ref[:, j * slots : (j + 1) * slots] = part.astype(F32).T.astype(BF)

    def gather(g, carry):
        pick = ones_at(k_ref[g], iota((table, rows), 0))
        got_ref[g] = dot(tab_ref[...], pick).astype(BF)
        return carry

    some = groups // sems.shape[0]
    copies = []
    for p in range(sems.shape[0]):
        lax.fori_loop(p * some, (p + 1) * some, gather, 0, unroll=GATHER_UNROLL)
        at = pl.ds(p * some, some)
        copies.append(pltpu.make_async_copy(got_ref.at[at], got_far.at[at], sems.at[p]))
        copies[p].start()
    for copy in copies:
        copy.wait()


def fore_kernel(
    which_ref,
    bar_ref,
    w_far,
    got_far,
    wbil_far,
    cot_far,
    term_ref,
    sum_ref,
    sems,
    w_ref,
    got_ref,
    wbil_ref,
    cot_ref,
    _,
    __,
    wbil_sem,
    cot_sem,
):
    groups, width, _ = got_ref.shape
    basis, edges, _ = sum_ref.shape
    stages = sems.shape[1]
    some = groups // stages
    staged = []
    for p in range(stages):
        at = pl.ds(p * some, some)
        staged.append(
            (
                pltpu.make_async_copy(w_far.at[at], w_ref.at[at], sems.at[0, p]),
                pltpu.make_async_copy(got_far.at[at], got_ref.at[at], sems.at[1, p]),
            )
        )
        for copy in staged[p]:
            copy.start()
    fetch_wbil = pltpu.make_async_copy(wbil_far, wbil_ref, wbil_sem)
    fetch_cot = pltpu.make_async_copy(cot_far, cot_ref, cot_sem)
    fetch_wbil.start()
    fetch_cot.start()
    for g in range(groups):
        if g % some == 0:
            for copy in staged[g // some]:
                copy.wait()
        total = dot(diagonal(w_ref[g]), got_ref[g], NT).astype(BF)
        sum_ref[:, g * GROUP : (g + 1) * GROUP, :] = total.reshape(basis, GROUP, width)
    fetch_wbil.wait()
    fetch_cot.wait()
    agg = jnp.zeros((width, edges), F32)
    for b in range(0, basis, 2):
        pair = jnp.concatenate([sum_ref[b], sum_ref[b + 1]], axis=1)
        agg = agg + dot(wbil_ref[:, b * width : (b + 2) * width], pair, NT)
    agg = agg.astype(BF)
    bar = bar_ref[...]
    own = term_ref.shape[0] // width - cot_ref.shape[1] // width
    for j in range(own):
        part = dot(sum_ref[which_ref[0] * own + j], bar, TN)
        term_ref[j * width : (j + 1) * width, :] = part.astype(BF)
    for h in range(cot_ref.shape[1] // width):
        up = dot(agg, cot_ref[:, h * width : (h + 1) * width])
        term_ref[(own + h) * width : (own + h + 1) * width, :] = up.astype(BF)


def last_kernel(got_ref, pre_ref, send_ref, wdown_ref, cot_ref, feats_ref, grad_ref, term_ref):
    edges, _ = cot_ref.shape
    share = edges // got_ref.shape[0]
    feats = got_ref.shape[0]
    part = lambda j: [got_ref[f, j * share : (j + 1) * share, :] for f in range(feats)]
    blocks = part(1) + part(2)
    count = send_ref.shape[1] // share
    total = jnp.concatenate(part(0), axis=0).astype(F32)
    place = ones_where(send_ref[...] == iota((edges, count * share), 0))
    total = total + dot(place, jnp.concatenate(blocks[:count], axis=0))
    pre_bar = (total * silu_grad(pre_ref[...])).astype(BF)
    grad_ref[...] = (cot_ref[...].astype(F32) + dot(pre_bar, wdown_ref[...], NT)).astype(BF)
    term_ref[...] = dot(feats_ref[...], pre_bar, TN).astype(BF)


def out_kernel(factor, total_ref, down_ref, up_ref, bil_ref):
    pieces, rows, width = total_ref.shape
    late = down_ref.shape[0] // pieces
    early = rows - late
    full = total_ref[...].astype(F32) * factor
    down_ref[...] = full[:, early:, :].reshape(down_ref.shape)
    flat = full[:, :early, :].reshape(pieces * early, width)
    own = bil_ref.shape[0]
    bil_ref[...] = flat[:own, :]
    for h in range(up_ref.shape[1] // width):
        up_ref[:, h * width : (h + 1) * width] = flat[own + h * width : own + (h + 1) * width, :]


def moved(value, steps):
    domains, feats = lax.axis_size(DOM), lax.axis_size("feat")
    pairs = [
        (d * feats + f, (d + step) % domains * feats + f)
        for d in range(domains)
        for f, step in enumerate(steps[:feats])
        if step is not None
    ]
    return lax.ppermute(value, (*DOM, "feat"), pairs)


def scattered_sum(pieces, axis):
    arrived = lax.all_to_all(pieces, axis, 0, 0)
    return jnp.sum(arrived.astype(F32), axis=0).astype(BF)


def everywhere(value, axis):
    count = lax.axis_size(axis)
    copies = lax.optimization_barrier(jnp.broadcast_to(value[None], (count, *value.shape)))
    return lax.all_to_all(copies, axis, 0, 0)


def exchanged_sum(value, axis):
    return jnp.sum(everywhere(value, axis).astype(F32), axis=0).astype(BF)


def steps(edge_feats, cotangent, w_down, w_up, w_bil, basis, trip_k, trip_count, send_rows):
    edges, span = edge_feats.shape
    width = w_down.shape[1]
    trips, basis_total, _ = basis.shape
    _, blocks, slots = send_rows.shape
    reach = blocks // 2
    offsets = [j + 1 if j < reach else reach - j - 1 for j in range(blocks)]
    feats = lax.axis_size("feat")
    groups = edges // GROUP
    own_basis = basis_total // feats
    low = lambda *shape: jax.ShapeDtypeStruct(shape, BF)
    feat = lax.axis_index("feat").astype(jnp.int32)
    which = feat.reshape(1)
    sends = offsets[:feats], (offsets[feats:] + [None] * feats)[:feats]
    backs = [[None if o is None else -o for o in steps] for steps in sends]

    both = call(
        first_kernel,
        low(feats, 2 * edges, width),
        [pltpu.VMEM((2 * edges, width), BF), pltpu.SemaphoreType.DMA((2, feats))],
        4 * edges * span * width,
        (),
        late=(edge_feats, w_down, cotangent, w_up),
        out_specs=pl.BlockSpec(memory_space=pltpu.HBM),
    )
    both = lax.all_to_all(both, "feat", 0, 0)

    by_basis, by_trip, turned = call(
        prep_kernel,
        [
            jax.ShapeDtypeStruct((groups, basis_total, trips * GROUP), F32),
            jax.ShapeDtypeStruct((groups, trips, basis_total * GROUP), F32),
            low(width, basis_total * width),
        ],
        [pltpu.VMEM((trips * basis_total, LANES), F32)],
        1 << 28,
        (),
        basis.reshape(trips * basis_total, edges),
        trip_count.reshape(1, edges),
        w_bil,
    )
    k_rows = trip_k.T.reshape(trips, groups, GROUP).transpose(1, 0, 2).reshape(groups, 1, -1)

    second = jnp.minimum(feats + feat, blocks - 1)
    listed = jnp.concatenate([send_rows[0, feat], send_rows[0, second]]).reshape(-1, 1)
    pre, bar, down, out_a, out_b = call(
        down_kernel,
        [
            jax.ShapeDtypeStruct((edges, width), F32),
            low(edges, width),
            low(edges, width),
            low(slots, width),
            low(slots, width),
        ],
        [],
        4 * slots * edges * width,
        (),
        both,
        listed,
    )
    in_a, in_b = moved(out_a, sends[0]), moved(out_b, sends[1])

    table = edges + blocks * slots
    big = 2 * edges * trips * width * 2000
    own, rem_a, rem_b = call(
        back_kernel,
        [low(slots, width)] * 3,
        [
            pltpu.VMEM((basis_total, edges, width), BF),
            pltpu.VMEM((3 * slots, width), F32),
            pltpu.SemaphoreType.DMA((len(CHUNKS),)),
        ],
        big,
        which,
        bar,
        k_rows,
        late=(by_trip, w_bil),
    )
    back_a = moved(rem_a, backs[0])
    back_b = moved(rem_b, backs[1])

    incoming, own = lax.optimization_barrier((jnp.concatenate([in_a, in_b], axis=0), own))
    incoming = everywhere(incoming, "feat")
    shared = everywhere(jnp.concatenate([own, back_a, back_b], axis=0), "feat")
    got = call(
        gather_kernel,
        pltpu.HBM((groups, width, trips * GROUP), BF),
        [
            pltpu.VMEM((width, table), BF),
            pltpu.VMEM((groups, width, trips * GROUP), BF),
            pltpu.SemaphoreType.DMA((4,)),
        ],
        big // 2,
        (),
        down,
        incoming,
        k_rows,
        out_specs=pl.BlockSpec(memory_space=pltpu.HBM),
    )
    early = call(
        fore_kernel,
        low(own_basis * width + span, width),
        [pltpu.VMEM((basis_total, edges, width), BF), pltpu.SemaphoreType.DMA((2, STAGES))],
        big,
        which,
        bar,
        late=(by_basis, got, turned, cotangent),
    )
    input_grad, late = call(
        last_kernel,
        [low(edges, span), low(span, width)],
        [],
        2 * edges * width * (blocks * slots + 3 * span),
        (),
        shared,
        pre,
        send_rows.reshape(1, -1),
        w_down,
        cotangent,
        edge_feats,
    )

    near = ("zl", "y", "core")
    count = lax.axis_size(near)
    pieces = [early.reshape(count, -1, width), late.reshape(count, -1, width)]
    total = scattered_sum(jnp.concatenate(pieces, axis=1), near)
    total = exchanged_sum(total, "zh")
    total = everywhere(total, near)
    factor = 1.0 / math.sqrt(edges * lax.axis_size(DOM))
    down_grad, up_grad, bil_grad = call(
        functools.partial(out_kernel, factor),
        [
            jax.ShapeDtypeStruct((span, width), F32),
            jax.ShapeDtypeStruct((width, span), F32),
            jax.ShapeDtypeStruct((own_basis * width, width), F32),
        ],
        [],
        1 << 20,
        (),
        total,
    )
    return input_grad, down_grad, up_grad, bil_grad


def solution(mesh):
    fine = Mesh(mesh.devices.reshape(8, 2, 4, 2, 4), (*DOM, "feat"))
    return jax.shard_map(
        steps,
        mesh=fine,
        in_specs=(
            P(DOM, "feat"),
            P(DOM, "feat"),
            P("feat", None),
            P(None, "feat"),
            P(),
            P(None, None, DOM),
            P(DOM, None),
            P(DOM),
            P(DOM, None, None),
        ),
        out_specs=(P(DOM, "feat"), P("feat", None), P(None, "feat"), P("feat", None)),
        check_vma=False,
    )
```

```python
import functools
import math

import jax
import jax.numpy as jnp
from jax import lax
from jax.experimental import pallas as pl
from jax.experimental.pallas import tpu as pltpu
from jax.sharding import Mesh
from jax.sharding import PartitionSpec as P

BF = jnp.bfloat16
F32 = jnp.float32
NT = (((1,), (1,)), ((), ()))
TN = (((0,), (0,)), ((), ()))
DOM = ("zh", "zl", "y", "core")
LANES = 128
CHUNKS = (0, 4, 8, 16)
STAGES = 8
GATHER_UNROLL = 4
VMEM_BYTES = 20 << 20
GROUP = 16


PLAIN = (((1,), (0,)), ((), ()))


def dot(a, b, dims=PLAIN):
    return lax.dot_general(a, b, dims, preferred_element_type=F32)


def ones_where(cond):
    return jnp.where(cond, 1.0, 0.0).astype(BF)


def ones_at(row, targets):
    rows = jnp.broadcast_to(row, targets.shape).astype(jnp.int16)
    return jnp.where(rows == targets.astype(jnp.int16), jnp.ones((), BF), jnp.zeros((), BF))


def iota(shape, dim):
    return lax.broadcasted_iota(jnp.int32, shape, dim)


def silu_grad(value):
    sigma = jax.nn.sigmoid(value)
    return sigma * (1.0 + value * (1.0 - sigma))


def call(kernel, outs, scratch, flops, which, *args, late=(), **more):
    moved_bytes = sum(a.size * a.dtype.itemsize for a in args)
    scalars = [pl.BlockSpec(memory_space=pltpu.SMEM)] if len(which) else []
    return pl.pallas_call(
        kernel,
        in_specs=scalars
        + [pl.BlockSpec(memory_space=pltpu.VMEM)] * len(args)
        + [pl.BlockSpec(memory_space=pltpu.HBM)] * len(late),
        out_shape=outs,
        **more,
        scratch_shapes=scratch
        + [pltpu.VMEM(a.shape, a.dtype) for a in late]
        + [pltpu.SemaphoreType.DMA] * len(late),
        compiler_params=pltpu.CompilerParams(vmem_limit_bytes=VMEM_BYTES),
        cost_estimate=pl.CostEstimate(flops=flops, bytes_accessed=moved_bytes, transcendentals=0),
    )(*([which] if len(which) else []), *args, *(pltpu.with_memory_space_constraint(a, pltpu.HBM) for a in late))


def first_kernel(feats_far, wdown_far, cot_far, wup_far, out_far, both_ref, sems, *fetched):
    refs, in_sems = fetched[:4], fetched[4:]
    fars = feats_far, wdown_far, cot_far, wup_far
    fetches = [pltpu.make_async_copy(*trio) for trio in zip(fars, refs, in_sems)]
    for fetch in fetches:
        fetch.start()
    count, rows, _ = out_far.shape
    half = rows // 2
    copies = []
    for h, dims in enumerate((PLAIN, NT)):
        fetches[2 * h].wait()
        fetches[2 * h + 1].wait()
        part = pl.ds(h * half, half)
        both_ref[part, :] = dot(refs[2 * h][...], refs[2 * h + 1][...], dims).astype(BF)
        for f in range(count):
            far = out_far.at[f, part]
            copies.append(pltpu.make_async_copy(both_ref.at[part], far, sems.at[h, f]))
            copies[-1].start()
    for copy in copies:
        copy.wait()


def summed_over(parts_ref, rows):
    total = parts_ref[0, rows, :].astype(F32)
    for f in range(1, parts_ref.shape[0]):
        total = total + parts_ref[f, rows, :].astype(F32)
    return total


def down_kernel(parts_ref, send_ref, pre_ref, bar_ref, down_ref, *out_refs):
    edges = pre_ref.shape[0]
    pre = summed_over(parts_ref, pl.ds(0, edges))
    pre_ref[...] = pre
    bar_ref[...] = summed_over(parts_ref, pl.ds(edges, edges)).astype(BF)
    down = (pre * jax.nn.sigmoid(pre)).astype(BF)
    down_ref[...] = down
    slots = out_refs[0].shape[0]
    for j, out_ref in enumerate(out_refs):
        pick = ones_where(send_ref[j * slots : (j + 1) * slots, :] == iota((slots, edges), 1))
        out_ref[...] = dot(pick, down).astype(BF)


def chunks_swapped(tiles):
    tiles = list(tiles)
    chunk = iota(tiles[0].shape, 1) // GROUP
    for step in (4, 2, 1):
        low = (chunk & step) == 0
        for i in range(8):
            if i & step:
                continue
            a, b = tiles[i], tiles[i + step]
            tiles[i] = jnp.where(low, a, pltpu.roll(b, GROUP * step, 1))
            tiles[i + step] = jnp.where(low, pltpu.roll(a, LANES - GROUP * step, 1), b)
    return tiles


def prep_kernel(basis_ref, count_ref, wbil_ref, by_basis_ref, by_trip_ref, turned_ref, live_ref):
    _, basis, _ = by_basis_ref.shape
    _, trips, _ = by_trip_ref.shape
    for t in range(count_ref.shape[1] // LANES):
        lanes = slice(t * LANES, (t + 1) * LANES)
        count = count_ref[:, lanes]
        tall = jnp.broadcast_to(count, (basis, LANES))
        for h in range(trips // 8):
            tiles = []
            for i in range(8 * h, 8 * h + 8):
                at = slice(i * basis, (i + 1) * basis)
                tiles.append(jnp.where(tall > i, basis_ref[at, lanes], 0.0))
                live_ref[at, :] = tiles[-1]
            for q, tile in enumerate(chunks_swapped(tiles)):
                by_basis_ref[8 * t + q, :, h * LANES : (h + 1) * LANES] = tile.astype(BF)
        for o in range(basis // 8):
            octet = range(8 * o, 8 * o + 8)
            tiles = [live_ref[pl.ds(b, trips, stride=basis), :] for b in octet]
            for q, tile in enumerate(chunks_swapped(tiles)):
                by_trip_ref[8 * t + q, :, o * LANES : (o + 1) * LANES] = tile.astype(BF)
    for b in range(basis):
        block = slice(b * LANES, (b + 1) * LANES)
        turned_ref[:, block] = wbil_ref[block, :].astype(F32).T.astype(BF)


def diagonal(rows):
    rows = rows.astype(F32)
    count, lanes = rows.shape
    same = iota((GROUP, lanes), 0) == iota((GROUP, lanes), 1) % GROUP
    parts = []
    for r in range(count):
        wide = jnp.broadcast_to(rows[r : r + 1, :], (GROUP, lanes))
        parts.append(jnp.where(same, wide, 0.0).astype(BF))
    return jnp.concatenate(parts, axis=0)


def back_kernel(
    which_ref,
    bar_ref,
    k_ref,
    w_far,
    wbil_far,
    own_ref,
    rem_a_ref,
    rem_b_ref,
    grad_ref,
    acc_ref,
    part_sems,
    w_sems,
    w_ref,
    wbil_ref,
    _,
    __,
):
    basis, edges, width = grad_ref.shape
    rows = k_ref.shape[2]
    slots = own_ref.shape[0]
    fetches = {}
    for p, (b, stop) in enumerate(zip(CHUNKS, (*CHUNKS[1:], basis))):
        at = pl.ds(b * width, (stop - b) * width)
        fetches[b] = pltpu.make_async_copy(wbil_far.at[at], wbil_ref.at[at], part_sems.at[p])
        fetches[b].start()
    groups = edges // GROUP
    some = groups // w_sems.shape[0]
    staged = []
    for p in range(groups // some):
        at = pl.ds(p * some, some)
        staged.append(pltpu.make_async_copy(w_far.at[at], w_ref.at[at], w_sems.at[p]))
        staged[p].start()
    bar = bar_ref[...]
    for b in range(basis):
        if b in fetches:
            fetches[b].wait()
        grad_ref[b] = dot(bar, wbil_ref[b * width : (b + 1) * width, :], NT).astype(BF)
    acc_ref[...] = jnp.zeros_like(acc_ref)
    first = which_ref[0] * slots
    row = iota((3 * slots, rows), 0)
    block = row // slots
    jump = jnp.where(block == 0, 0, edges + (block - 1) * 4 * slots - block * slots)
    target = row + jump
    for g in range(groups):
        if g % some == 0:
            staged[g // some].wait()
        grad = grad_ref[:, g * GROUP : (g + 1) * GROUP, :].reshape(basis * GROUP, width)
        d_rows = dot(diagonal(w_ref[g]), grad).astype(BF)
        acc_ref[...] += dot(ones_at(k_ref[g] - first, target), d_rows)
    for j, ref in enumerate((own_ref, rem_a_ref, rem_b_ref)):
        ref[...] = acc_ref[j * slots : (j + 1) * slots, :].astype(BF)


def gather_kernel(down_ref, in_ref, k_ref, got_far, tab_ref, got_ref, sems):
    groups, _, rows = got_ref.shape
    edges = down_ref.shape[0]
    table = tab_ref.shape[1]
    slots = in_ref.shape[1] // 2
    parts = [down_ref[j * slots : (j + 1) * slots, :] for j in range(edges // slots)]
    parts += [in_ref[f, :slots, :] for f in range(4)] + [in_ref[f, slots:, :] for f in range(2)]
    for j, part in enumerate(parts):
        tab_ref[:, j * slots : (j + 1) * slots] = part.astype(F32).T.astype(BF)

    def gather(g, carry):
        pick = ones_at(k_ref[g], iota((table, rows), 0))
        got_ref[g] = dot(tab_ref[...], pick).astype(BF)
        return carry

    some = groups // sems.shape[0]
    copies = []
    for p in range(sems.shape[0]):
        lax.fori_loop(p * some, (p + 1) * some, gather, 0, unroll=GATHER_UNROLL)
        at = pl.ds(p * some, some)
        copies.append(pltpu.make_async_copy(got_ref.at[at], got_far.at[at], sems.at[p]))
        copies[p].start()
    for copy in copies:
        copy.wait()


def fore_kernel(
    which_ref,
    bar_ref,
    w_far,
    got_far,
    wbil_far,
    cot_far,
    term_ref,
    sum_ref,
    sems,
    w_ref,
    got_ref,
    wbil_ref,
    cot_ref,
    _,
    __,
    wbil_sem,
    cot_sem,
):
    groups, width, _ = got_ref.shape
    basis, edges, _ = sum_ref.shape
    stages = sems.shape[1]
    some = groups // stages
    staged = []
    for p in range(stages):
        at = pl.ds(p * some, some)
        staged.append(
            (
                pltpu.make_async_copy(w_far.at[at], w_ref.at[at], sems.at[0, p]),
                pltpu.make_async_copy(got_far.at[at], got_ref.at[at], sems.at[1, p]),
            )
        )
        for copy in staged[p]:
            copy.start()
    fetch_wbil = pltpu.make_async_copy(wbil_far, wbil_ref, wbil_sem)
    fetch_cot = pltpu.make_async_copy(cot_far, cot_ref, cot_sem)
    fetch_wbil.start()
    fetch_cot.start()
    for g in range(groups):
        if g % some == 0:
            for copy in staged[g // some]:
                copy.wait()
        total = dot(diagonal(w_ref[g]), got_ref[g], NT).astype(BF)
        sum_ref[:, g * GROUP : (g + 1) * GROUP, :] = total.reshape(basis, GROUP, width)
    fetch_wbil.wait()
    fetch_cot.wait()
    agg = jnp.zeros((width, edges), F32)
    for b in range(0, basis, 2):
        pair = jnp.concatenate([sum_ref[b], sum_ref[b + 1]], axis=1)
        agg = agg + dot(wbil_ref[:, b * width : (b + 2) * width], pair, NT)
    agg = agg.astype(BF)
    bar = bar_ref[...]
    own = term_ref.shape[0] // width - cot_ref.shape[1] // width
    for j in range(own):
        part = dot(sum_ref[which_ref[0] * own + j], bar, TN)
        term_ref[j * width : (j + 1) * width, :] = part.astype(BF)
    for h in range(cot_ref.shape[1] // width):
        up = dot(agg, cot_ref[:, h * width : (h + 1) * width])
        term_ref[(own + h) * width : (own + h + 1) * width, :] = up.astype(BF)


def last_kernel(got_ref, pre_ref, send_ref, wdown_ref, cot_ref, feats_ref, grad_ref, term_ref):
    edges, _ = cot_ref.shape
    share = edges // got_ref.shape[0]
    feats = got_ref.shape[0]
    part = lambda j: [got_ref[f, j * share : (j + 1) * share, :] for f in range(feats)]
    blocks = part(1) + part(2)
    count = send_ref.shape[1] // share
    total = jnp.concatenate(part(0), axis=0).astype(F32)
    place = ones_where(send_ref[...] == iota((edges, count * share), 0))
    total = total + dot(place, jnp.concatenate(blocks[:count], axis=0))
    pre_bar = (total * silu_grad(pre_ref[...])).astype(BF)
    grad_ref[...] = (cot_ref[...].astype(F32) + dot(pre_bar, wdown_ref[...], NT)).astype(BF)
    term_ref[...] = dot(feats_ref[...], pre_bar, TN).astype(BF)


def out_kernel(factor, total_ref, down_ref, up_ref, bil_ref):
    pieces, rows, width = total_ref.shape
    late = down_ref.shape[0] // pieces
    early = rows - late
    full = total_ref[...].astype(F32) * factor
    down_ref[...] = full[:, early:, :].reshape(down_ref.shape)
    flat = full[:, :early, :].reshape(pieces * early, width)
    own = bil_ref.shape[0]
    bil_ref[...] = flat[:own, :]
    for h in range(up_ref.shape[1] // width):
        up_ref[:, h * width : (h + 1) * width] = flat[own + h * width : own + (h + 1) * width, :]


def moved(value, steps):
    domains, feats = lax.axis_size(DOM), lax.axis_size("feat")
    pairs = [
        (d * feats + f, (d + step) % domains * feats + f)
        for d in range(domains)
        for f, step in enumerate(steps[:feats])
        if step is not None
    ]
    return lax.ppermute(value, (*DOM, "feat"), pairs)


def scattered_sum(pieces, axis):
    arrived = lax.all_to_all(pieces, axis, 0, 0)
    return jnp.sum(arrived.astype(F32), axis=0).astype(BF)


def everywhere(value, axis):
    count = lax.axis_size(axis)
    copies = lax.optimization_barrier(jnp.broadcast_to(value[None], (count, *value.shape)))
    return lax.all_to_all(copies, axis, 0, 0)


def exchanged_sum(value, axis):
    return jnp.sum(everywhere(value, axis).astype(F32), axis=0).astype(BF)


def steps(edge_feats, cotangent, w_down, w_up, w_bil, basis, trip_k, trip_count, send_rows):
    edges, span = edge_feats.shape
    width = w_down.shape[1]
    trips, basis_total, _ = basis.shape
    _, blocks, slots = send_rows.shape
    reach = blocks // 2
    offsets = [j + 1 if j < reach else reach - j - 1 for j in range(blocks)]
    feats = lax.axis_size("feat")
    groups = edges // GROUP
    own_basis = basis_total // feats
    low = lambda *shape: jax.ShapeDtypeStruct(shape, BF)
    feat = lax.axis_index("feat").astype(jnp.int32)
    which = feat.reshape(1)
    sends = offsets[:feats], (offsets[feats:] + [None] * feats)[:feats]
    backs = [[None if o is None else -o for o in steps] for steps in sends]

    both = call(
        first_kernel,
        low(feats, 2 * edges, width),
        [pltpu.VMEM((2 * edges, width), BF), pltpu.SemaphoreType.DMA((2, feats))],
        4 * edges * span * width,
        (),
        late=(edge_feats, w_down, cotangent, w_up),
        out_specs=pl.BlockSpec(memory_space=pltpu.HBM),
    )
    both = lax.all_to_all(both, "feat", 0, 0)

    by_basis, by_trip, turned = call(
        prep_kernel,
        [
            low(groups, basis_total, trips * GROUP),
            low(groups, trips, basis_total * GROUP),
            low(width, basis_total * width),
        ],
        [pltpu.VMEM((trips * basis_total, LANES), F32)],
        1 << 28,
        (),
        basis.reshape(trips * basis_total, edges),
        trip_count.reshape(1, edges),
        w_bil,
    )
    k_rows = trip_k.T.reshape(trips, groups, GROUP).transpose(1, 0, 2).reshape(groups, 1, -1)

    second = jnp.minimum(feats + feat, blocks - 1)
    listed = jnp.concatenate([send_rows[0, feat], send_rows[0, second]]).reshape(-1, 1)
    pre, bar, down, out_a, out_b = call(
        down_kernel,
        [
            jax.ShapeDtypeStruct((edges, width), F32),
            low(edges, width),
            low(edges, width),
            low(slots, width),
            low(slots, width),
        ],
        [],
        4 * slots * edges * width,
        (),
        both,
        listed,
    )
    in_a, in_b = moved(out_a, sends[0]), moved(out_b, sends[1])

    table = edges + blocks * slots
    big = 2 * edges * trips * width * 2000
    own, rem_a, rem_b = call(
        back_kernel,
        [low(slots, width)] * 3,
        [
            pltpu.VMEM((basis_total, edges, width), BF),
            pltpu.VMEM((3 * slots, width), F32),
            pltpu.SemaphoreType.DMA((len(CHUNKS),)),
            pltpu.SemaphoreType.DMA((STAGES,)),
        ],
        big,
        which,
        bar,
        k_rows,
        late=(by_trip, w_bil),
    )
    back_a = moved(rem_a, backs[0])
    back_b = moved(rem_b, backs[1])

    incoming, own = lax.optimization_barrier((jnp.concatenate([in_a, in_b], axis=0), own))
    incoming = everywhere(incoming, "feat")
    shared = everywhere(jnp.concatenate([own, back_a, back_b], axis=0), "feat")
    got = call(
        gather_kernel,
        pltpu.HBM((groups, width, trips * GROUP), BF),
        [
            pltpu.VMEM((width, table), BF),
            pltpu.VMEM((groups, width, trips * GROUP), BF),
            pltpu.SemaphoreType.DMA((STAGES,)),
        ],
        big // 2,
        (),
        down,
        incoming,
        k_rows,
        out_specs=pl.BlockSpec(memory_space=pltpu.HBM),
    )
    early = call(
        fore_kernel,
        low(own_basis * width + span, width),
        [pltpu.VMEM((basis_total, edges, width), BF), pltpu.SemaphoreType.DMA((2, STAGES))],
        big,
        which,
        bar,
        late=(by_basis, got, turned, cotangent),
    )
    input_grad, late = call(
        last_kernel,
        [low(edges, span), low(span, width)],
        [],
        2 * edges * width * (blocks * slots + 3 * span),
        (),
        shared,
        pre,
        send_rows.reshape(1, -1),
        w_down,
        cotangent,
        edge_feats,
    )

    near = ("zl", "y", "core")
    count = lax.axis_size(near)
    pieces = [early.reshape(count, -1, width), late.reshape(count, -1, width)]
    total = scattered_sum(jnp.concatenate(pieces, axis=1), near)
    total = exchanged_sum(total, "zh")
    total = everywhere(total, near)
    factor = 1.0 / math.sqrt(edges * lax.axis_size(DOM))
    down_grad, up_grad, bil_grad = call(
        functools.partial(out_kernel, factor),
        [
            jax.ShapeDtypeStruct((span, width), F32),
            jax.ShapeDtypeStruct((width, span), F32),
            jax.ShapeDtypeStruct((own_basis * width, width), F32),
        ],
        [],
        1 << 20,
        (),
        total,
    )
    return input_grad, down_grad, up_grad, bil_grad


def solution(mesh):
    fine = Mesh(mesh.devices.reshape(8, 2, 4, 2, 4), (*DOM, "feat"))
    return jax.shard_map(
        steps,
        mesh=fine,
        in_specs=(
            P(DOM, "feat"),
            P(DOM, "feat"),
            P("feat", None),
            P(None, "feat"),
            P(),
            P(None, None, DOM),
            P(DOM, None),
            P(DOM),
            P(DOM, None, None),
        ),
        out_specs=(P(DOM, "feat"), P("feat", None), P(None, "feat"), P("feat", None)),
        check_vma=False,
    )
```

```python
import functools
import math

import jax
import jax.numpy as jnp
from jax import lax
from jax.experimental import pallas as pl
from jax.experimental.pallas import tpu as pltpu
from jax.sharding import Mesh
from jax.sharding import PartitionSpec as P

BF = jnp.bfloat16
F32 = jnp.float32
NT = (((1,), (1,)), ((), ()))
TN = (((0,), (0,)), ((), ()))
DOM = ("zh", "zl", "y", "core")
LANES = 128
CHUNKS = (0, 4, 8, 16)
STAGES = 8
HALVES = 2
UNROLL = 4
GATHER_UNROLL = 4
VMEM_BYTES = 20 << 20
GROUP = 16


PLAIN = (((1,), (0,)), ((), ()))


def dot(a, b, dims=PLAIN):
    return lax.dot_general(a, b, dims, preferred_element_type=F32)


def ones_where(cond):
    return jnp.where(cond, 1.0, 0.0).astype(BF)


def ones_at(row, targets):
    rows = jnp.broadcast_to(row, targets.shape).astype(jnp.int16)
    return jnp.where(rows == targets.astype(jnp.int16), jnp.ones((), BF), jnp.zeros((), BF))


def iota(shape, dim):
    return lax.broadcasted_iota(jnp.int32, shape, dim)


def silu_grad(value):
    sigma = jax.nn.sigmoid(value)
    return sigma * (1.0 + value * (1.0 - sigma))


def call(kernel, outs, scratch, flops, which, *args, late=(), **more):
    moved_bytes = sum(a.size * a.dtype.itemsize for a in args)
    scalars = [pl.BlockSpec(memory_space=pltpu.SMEM)] if len(which) else []
    return pl.pallas_call(
        kernel,
        in_specs=scalars
        + [pl.BlockSpec(memory_space=pltpu.VMEM)] * len(args)
        + [pl.BlockSpec(memory_space=pltpu.HBM)] * len(late),
        out_shape=outs,
        **more,
        scratch_shapes=scratch
        + [pltpu.VMEM(a.shape, a.dtype) for a in late]
        + [pltpu.SemaphoreType.DMA] * len(late),
        compiler_params=pltpu.CompilerParams(vmem_limit_bytes=VMEM_BYTES),
        cost_estimate=pl.CostEstimate(flops=flops, bytes_accessed=moved_bytes, transcendentals=0),
    )(*([which] if len(which) else []), *args, *(pltpu.with_memory_space_constraint(a, pltpu.HBM) for a in late))


def first_kernel(feats_far, wdown_far, cot_far, wup_far, out_far, both_ref, sems, *fetched):
    refs, in_sems = fetched[:4], fetched[4:]
    fars = feats_far, wdown_far, cot_far, wup_far
    fetches = [pltpu.make_async_copy(*trio) for trio in zip(fars, refs, in_sems)]
    for fetch in fetches:
        fetch.start()
    count, rows, _ = out_far.shape
    half = rows // 2
    copies = []
    for h, dims in enumerate((PLAIN, NT)):
        fetches[2 * h].wait()
        fetches[2 * h + 1].wait()
        part = pl.ds(h * half, half)
        both_ref[part, :] = dot(refs[2 * h][...], refs[2 * h + 1][...], dims).astype(BF)
        for f in range(count):
            far = out_far.at[f, part]
            copies.append(pltpu.make_async_copy(both_ref.at[part], far, sems.at[h, f]))
            copies[-1].start()
    for copy in copies:
        copy.wait()


def summed_over(parts_ref, rows):
    total = parts_ref[0, rows, :].astype(F32)
    for f in range(1, parts_ref.shape[0]):
        total = total + parts_ref[f, rows, :].astype(F32)
    return total


def down_kernel(parts_ref, send_ref, pre_ref, bar_ref, down_ref, *out_refs):
    edges = pre_ref.shape[0]
    pre = summed_over(parts_ref, pl.ds(0, edges))
    pre_ref[...] = pre
    bar_ref[...] = summed_over(parts_ref, pl.ds(edges, edges)).astype(BF)
    down = (pre * jax.nn.sigmoid(pre)).astype(BF)
    down_ref[...] = down
    slots = out_refs[0].shape[0]
    for j, out_ref in enumerate(out_refs):
        pick = ones_where(send_ref[j * slots : (j + 1) * slots, :] == iota((slots, edges), 1))
        out_ref[...] = dot(pick, down).astype(BF)


def chunks_swapped(tiles):
    tiles = list(tiles)
    chunk = iota(tiles[0].shape, 1) // GROUP
    for step in (4, 2, 1):
        low = (chunk & step) == 0
        for i in range(8):
            if i & step:
                continue
            a, b = tiles[i], tiles[i + step]
            tiles[i] = jnp.where(low, a, pltpu.roll(b, GROUP * step, 1))
            tiles[i + step] = jnp.where(low, pltpu.roll(a, LANES - GROUP * step, 1), b)
    return tiles


def prep_kernel(basis_ref, count_ref, wbil_ref, by_basis_ref, by_trip_ref, turned_ref, live_ref):
    _, basis, _ = by_basis_ref.shape
    _, trips, _ = by_trip_ref.shape
    for t in range(count_ref.shape[1] // LANES):
        lanes = slice(t * LANES, (t + 1) * LANES)
        count = count_ref[:, lanes]
        tall = jnp.broadcast_to(count, (basis, LANES))
        for h in range(trips // 8):
            tiles = []
            for i in range(8 * h, 8 * h + 8):
                at = slice(i * basis, (i + 1) * basis)
                tiles.append(jnp.where(tall > i, basis_ref[at, lanes], 0.0))
                live_ref[at, :] = tiles[-1]
            for q, tile in enumerate(chunks_swapped(tiles)):
                by_basis_ref[8 * t + q, :, h * LANES : (h + 1) * LANES] = tile.astype(BF)
        for o in range(basis // 8):
            octet = range(8 * o, 8 * o + 8)
            tiles = [live_ref[pl.ds(b, trips, stride=basis), :] for b in octet]
            for q, tile in enumerate(chunks_swapped(tiles)):
                by_trip_ref[8 * t + q, :, o * LANES : (o + 1) * LANES] = tile.astype(BF)
    for b in range(basis):
        block = slice(b * LANES, (b + 1) * LANES)
        turned_ref[:, block] = wbil_ref[block, :].astype(F32).T.astype(BF)


def diagonal(rows):
    rows = rows.astype(F32)
    count, lanes = rows.shape
    same = iota((GROUP, lanes), 0) == iota((GROUP, lanes), 1) % GROUP
    parts = []
    for r in range(count):
        wide = jnp.broadcast_to(rows[r : r + 1, :], (GROUP, lanes))
        parts.append(jnp.where(same, wide, 0.0).astype(BF))
    return jnp.concatenate(parts, axis=0)


def back_kernel(
    which_ref,
    bar_ref,
    k_ref,
    w_far,
    wbil_far,
    own_ref,
    rem_a_ref,
    rem_b_ref,
    grad_ref,
    acc_ref,
    part_sems,
    w_sems,
    w_ref,
    wbil_ref,
    _,
    __,
):
    basis, edges, width = grad_ref.shape
    rows = k_ref.shape[2]
    slots = own_ref.shape[0]
    fetches = {}
    for p, (b, stop) in enumerate(zip(CHUNKS, (*CHUNKS[1:], basis))):
        at = pl.ds(b * width, (stop - b) * width)
        fetches[b] = pltpu.make_async_copy(wbil_far.at[at], wbil_ref.at[at], part_sems.at[p])
        fetches[b].start()
    groups = edges // GROUP
    some = groups // w_sems.shape[0]
    staged = []
    for p in range(groups // some):
        at = pl.ds(p * some, some)
        staged.append(pltpu.make_async_copy(w_far.at[at], w_ref.at[at], w_sems.at[p]))
        staged[p].start()
    bar = bar_ref[...]
    for b in range(basis):
        if b in fetches:
            fetches[b].wait()
        grad_ref[b] = dot(bar, wbil_ref[b * width : (b + 1) * width, :], NT).astype(BF)
    acc_ref[...] = jnp.zeros_like(acc_ref)
    first = which_ref[0] * slots
    row = iota((3 * slots, rows), 0)
    block = row // slots
    jump = jnp.where(block == 0, 0, edges + (block - 1) * 4 * slots - block * slots)
    target = row + jump

    def body(g, carry):
        at = pl.ds(pl.multiple_of(g * GROUP, GROUP), GROUP)
        grad = grad_ref[:, at, :].reshape(basis * GROUP, width)
        d_rows = dot(diagonal(w_ref[g]), grad).astype(BF)
        acc_ref[...] += dot(ones_at(k_ref[g] - first, target), d_rows)
        return carry

    for p in range(groups // some):
        staged[p].wait()
        lax.fori_loop(p * some, (p + 1) * some, body, 0, unroll=UNROLL)
    for j, ref in enumerate((own_ref, rem_a_ref, rem_b_ref)):
        ref[...] = acc_ref[j * slots : (j + 1) * slots, :].astype(BF)


def gather_kernel(down_ref, in_ref, k_ref, got_far, tab_ref, got_ref, sems):
    groups, _, rows = got_ref.shape
    edges = down_ref.shape[0]
    table = tab_ref.shape[1]
    slots = in_ref.shape[1] // 2
    parts = [down_ref[j * slots : (j + 1) * slots, :] for j in range(edges // slots)]
    parts += [in_ref[f, :slots, :] for f in range(4)] + [in_ref[f, slots:, :] for f in range(2)]
    for j, part in enumerate(parts):
        tab_ref[:, j * slots : (j + 1) * slots] = part.astype(F32).T.astype(BF)

    def gather(g, carry):
        pick = ones_at(k_ref[g], iota((table, rows), 0))
        got_ref[g] = dot(tab_ref[...], pick).astype(BF)
        return carry

    some = groups // sems.shape[0]
    copies = []
    for p in range(sems.shape[0]):
        lax.fori_loop(p * some, (p + 1) * some, gather, 0, unroll=GATHER_UNROLL)
        at = pl.ds(p * some, some)
        copies.append(pltpu.make_async_copy(got_ref.at[at], got_far.at[at], sems.at[p]))
        copies[p].start()
    for copy in copies:
        copy.wait()


def fore_kernel(
    which_ref,
    bar_ref,
    w_far,
    got_far,
    wbil_far,
    cot_far,
    term_ref,
    sum_ref,
    sems,
    w_ref,
    got_ref,
    wbil_ref,
    cot_ref,
    _,
    __,
    wbil_sem,
    cot_sem,
):
    groups, width, _ = got_ref.shape
    basis, edges, _ = sum_ref.shape
    stages = sems.shape[1]
    some = groups // stages
    staged = []
    for p in range(stages):
        at = pl.ds(p * some, some)
        staged.append(
            (
                pltpu.make_async_copy(w_far.at[at], w_ref.at[at], sems.at[0, p]),
                pltpu.make_async_copy(got_far.at[at], got_ref.at[at], sems.at[1, p]),
            )
        )
        for copy in staged[p]:
            copy.start()
    fetch_wbil = pltpu.make_async_copy(wbil_far, wbil_ref, wbil_sem)
    fetch_cot = pltpu.make_async_copy(cot_far, cot_ref, cot_sem)
    fetch_wbil.start()
    fetch_cot.start()

    def add_up(g, carry):
        at = pl.ds(pl.multiple_of(g * GROUP, GROUP), GROUP)
        total = dot(diagonal(w_ref[g]), got_ref[g], NT).astype(BF)
        sum_ref[:, at, :] = total.reshape(basis, GROUP, width)
        return carry

    for p in range(stages):
        for copy in staged[p]:
            copy.wait()
        lax.fori_loop(p * some, (p + 1) * some, add_up, 0, unroll=UNROLL)
    fetch_wbil.wait()
    fetch_cot.wait()
    agg = jnp.zeros((width, edges), F32)
    for b in range(0, basis, 2):
        pair = jnp.concatenate([sum_ref[b], sum_ref[b + 1]], axis=1)
        agg = agg + dot(wbil_ref[:, b * width : (b + 2) * width], pair, NT)
    agg = agg.astype(BF)
    bar = bar_ref[...]
    own = term_ref.shape[0] // width - cot_ref.shape[1] // width
    for j in range(own):
        part = dot(sum_ref[which_ref[0] * own + j], bar, TN)
        term_ref[j * width : (j + 1) * width, :] = part.astype(BF)
    for h in range(cot_ref.shape[1] // width):
        up = dot(agg, cot_ref[:, h * width : (h + 1) * width])
        term_ref[(own + h) * width : (own + h + 1) * width, :] = up.astype(BF)


def last_kernel(got_ref, pre_ref, send_ref, wdown_ref, cot_ref, feats_ref, grad_ref, term_ref):
    edges, _ = cot_ref.shape
    share = edges // got_ref.shape[0]
    feats = got_ref.shape[0]
    part = lambda j: [got_ref[f, j * share : (j + 1) * share, :] for f in range(feats)]
    blocks = part(1) + part(2)
    count = send_ref.shape[1] // share
    total = jnp.concatenate(part(0), axis=0).astype(F32)
    place = ones_where(send_ref[...] == iota((edges, count * share), 0))
    total = total + dot(place, jnp.concatenate(blocks[:count], axis=0))
    pre_bar = (total * silu_grad(pre_ref[...])).astype(BF)
    grad_ref[...] = (cot_ref[...].astype(F32) + dot(pre_bar, wdown_ref[...], NT)).astype(BF)
    term_ref[...] = dot(feats_ref[...], pre_bar, TN).astype(BF)


def out_kernel(factor, total_ref, down_ref, up_ref, bil_ref):
    pieces, rows, width = total_ref.shape
    late = down_ref.shape[0] // pieces
    early = rows - late
    full = total_ref[...].astype(F32) * factor
    down_ref[...] = full[:, early:, :].reshape(down_ref.shape)
    flat = full[:, :early, :].reshape(pieces * early, width)
    own = bil_ref.shape[0]
    bil_ref[...] = flat[:own, :]
    for h in range(up_ref.shape[1] // width):
        up_ref[:, h * width : (h + 1) * width] = flat[own + h * width : own + (h + 1) * width, :]


def moved(value, steps):
    domains, feats = lax.axis_size(DOM), lax.axis_size("feat")
    pairs = [
        (d * feats + f, (d + step) % domains * feats + f)
        for d in range(domains)
        for f, step in enumerate(steps[:feats])
        if step is not None
    ]
    return lax.ppermute(value, (*DOM, "feat"), pairs)


def scattered_sum(pieces, axis):
    arrived = lax.all_to_all(pieces, axis, 0, 0)
    return jnp.sum(arrived.astype(F32), axis=0).astype(BF)


def everywhere(value, axis):
    count = lax.axis_size(axis)
    copies = lax.optimization_barrier(jnp.broadcast_to(value[None], (count, *value.shape)))
    return lax.all_to_all(copies, axis, 0, 0)


def exchanged_sum(value, axis):
    return jnp.sum(everywhere(value, axis).astype(F32), axis=0).astype(BF)


def steps(edge_feats, cotangent, w_down, w_up, w_bil, basis, trip_k, trip_count, send_rows):
    edges, span = edge_feats.shape
    width = w_down.shape[1]
    trips, basis_total, _ = basis.shape
    _, blocks, slots = send_rows.shape
    reach = blocks // 2
    offsets = [j + 1 if j < reach else reach - j - 1 for j in range(blocks)]
    feats = lax.axis_size("feat")
    groups = edges // GROUP
    own_basis = basis_total // feats
    low = lambda *shape: jax.ShapeDtypeStruct(shape, BF)
    feat = lax.axis_index("feat").astype(jnp.int32)
    which = feat.reshape(1)
    sends = offsets[:feats], (offsets[feats:] + [None] * feats)[:feats]
    backs = [[None if o is None else -o for o in steps] for steps in sends]

    both = call(
        first_kernel,
        low(feats, 2 * edges, width),
        [pltpu.VMEM((2 * edges, width), BF), pltpu.SemaphoreType.DMA((2, feats))],
        4 * edges * span * width,
        (),
        late=(edge_feats, w_down, cotangent, w_up),
        out_specs=pl.BlockSpec(memory_space=pltpu.HBM),
    )
    both = lax.all_to_all(both, "feat", 0, 0)

    by_basis, by_trip, turned = call(
        prep_kernel,
        [
            low(groups, basis_total, trips * GROUP),
            low(groups, trips, basis_total * GROUP),
            low(width, basis_total * width),
        ],
        [pltpu.VMEM((trips * basis_total, LANES), F32)],
        1 << 28,
        (),
        basis.reshape(trips * basis_total, edges),
        trip_count.reshape(1, edges),
        w_bil,
    )
    k_rows = trip_k.T.reshape(trips, groups, GROUP).transpose(1, 0, 2).reshape(groups, 1, -1)

    second = jnp.minimum(feats + feat, blocks - 1)
    listed = jnp.concatenate([send_rows[0, feat], send_rows[0, second]]).reshape(-1, 1)
    pre, bar, down, out_a, out_b = call(
        down_kernel,
        [
            jax.ShapeDtypeStruct((edges, width), F32),
            low(edges, width),
            low(edges, width),
            low(slots, width),
            low(slots, width),
        ],
        [],
        4 * slots * edges * width,
        (),
        both,
        listed,
    )
    in_a, in_b = moved(out_a, sends[0]), moved(out_b, sends[1])

    table = edges + blocks * slots
    big = 2 * edges * trips * width * 2000
    own, rem_a, rem_b = call(
        back_kernel,
        [low(slots, width)] * 3,
        [
            pltpu.VMEM((basis_total, edges, width), BF),
            pltpu.VMEM((3 * slots, width), F32),
            pltpu.SemaphoreType.DMA((len(CHUNKS),)),
            pltpu.SemaphoreType.DMA((HALVES,)),
        ],
        big,
        which,
        bar,
        k_rows,
        late=(by_trip, w_bil),
    )
    back_a = moved(rem_a, backs[0])
    back_b = moved(rem_b, backs[1])

    incoming, own = lax.optimization_barrier((jnp.concatenate([in_a, in_b], axis=0), own))
    incoming = everywhere(incoming, "feat")
    shared = everywhere(jnp.concatenate([own, back_a, back_b], axis=0), "feat")
    got = call(
        gather_kernel,
        pltpu.HBM((groups, width, trips * GROUP), BF),
        [
            pltpu.VMEM((width, table), BF),
            pltpu.VMEM((groups, width, trips * GROUP), BF),
            pltpu.SemaphoreType.DMA((STAGES,)),
        ],
        big // 2,
        (),
        down,
        incoming,
        k_rows,
        out_specs=pl.BlockSpec(memory_space=pltpu.HBM),
    )
    early = call(
        fore_kernel,
        low(own_basis * width + span, width),
        [pltpu.VMEM((basis_total, edges, width), BF), pltpu.SemaphoreType.DMA((2, HALVES))],
        big,
        which,
        bar,
        late=(by_basis, got, turned, cotangent),
    )
    input_grad, late = call(
        last_kernel,
        [low(edges, span), low(span, width)],
        [],
        2 * edges * width * (blocks * slots + 3 * span),
        (),
        shared,
        pre,
        send_rows.reshape(1, -1),
        w_down,
        cotangent,
        edge_feats,
    )

    near = ("zl", "y", "core")
    count = lax.axis_size(near)
    pieces = [early.reshape(count, -1, width), late.reshape(count, -1, width)]
    total = scattered_sum(jnp.concatenate(pieces, axis=1), near)
    total = exchanged_sum(total, "zh")
    total = everywhere(total, near)
    factor = 1.0 / math.sqrt(edges * lax.axis_size(DOM))
    down_grad, up_grad, bil_grad = call(
        functools.partial(out_kernel, factor),
        [
            jax.ShapeDtypeStruct((span, width), F32),
            jax.ShapeDtypeStruct((width, span), F32),
            jax.ShapeDtypeStruct((own_basis * width, width), F32),
        ],
        [],
        1 << 20,
        (),
        total,
    )
    return input_grad, down_grad, up_grad, bil_grad


def solution(mesh):
    fine = Mesh(mesh.devices.reshape(8, 2, 4, 2, 4), (*DOM, "feat"))
    return jax.shard_map(
        steps,
        mesh=fine,
        in_specs=(
            P(DOM, "feat"),
            P(DOM, "feat"),
            P("feat", None),
            P(None, "feat"),
            P(),
            P(None, None, DOM),
            P(DOM, None),
            P(DOM),
            P(DOM, None, None),
        ),
        out_specs=(P(DOM, "feat"), P("feat", None), P(None, "feat"), P("feat", None)),
        check_vma=False,
    )
```
